32 devices in a mesh: ctx: 4 (over x, core), exp: 4 (over z), tp: 2 (over y).
Axes of the slice: x: 2, y: 2, z: 4, core: 2. Of those that a mesh axis runs over, the one named last changes fastest.
Arguments:
- mamba_in: bfloat16 [512, 8192], P('ctx', ('exp', 'tp')), may hold values from -6 to 6
- gate_in: bfloat16 [512, 8192], P('ctx', ('exp', 'tp')), may hold values from -6 to 6
- step_size: float32 [512, 8192], P('ctx', ('exp', 'tp')), may hold values from 0 to 2
- input_proj: float32 [16, 512], P(None, 'ctx'), may hold values from -6 to 6
- output_proj: float32 [16, 512], P(None, 'ctx'), may hold values from -6 to 6
- decay_log: float32 [16, 8192], P(None, ('exp', 'tp')), may hold values from -0.7 to 0.7
- skip_gain: float32 [8192], P(('exp', 'tp')), may hold values from 0.5 to 2
- out_weight: bfloat16 [8192, 2048], P(('exp', 'tp')), may hold values from -0.0625 to 0.0625
- residual: bfloat16 [512, 2048], P('ctx', ('exp', 'tp')), may hold values from -6 to 6
- routes: int32 [512, 2], P('ctx'), may hold values from 0 to 3, all different within a row; in each aligned block of 128 rows (0 to 127, 128 to 255, ...) at most 128 rows name the same one
- norm_gain: float32 [2048], replicated, may hold values from 0.25 to 1.75
- w_gate: bfloat16 [4, 2048, 14336], P('exp', None, ('ctx', 'tp')), may hold values from -0.125 to 0.125
- w_up: bfloat16 [4, 2048, 14336], P('exp', None, ('ctx', 'tp')), may hold values from -0.125 to 0.125
- w_down: bfloat16 [4, 14336, 2048], P('exp', 'ctx', 'tp'), may hold values from -0.046875 to 0.046875
Outputs:
- expert_out: bfloat16 [4, 4, 128, 2048], P('ctx', 'exp', None, 'tp')
The draws below stay inside these ranges and needn't reach their ends.
Inputs may be any that keep to these rules, and one draw needn't show every extreme that they name: `routes`: within each aligned block of 128 positions no expert is named by more than 128 of the block's rows, a bound that some expert reaches in some block.
All inputs are finite; a program needn't handle non-finite values.
Results may differ from the reference program's by a relative error of at most 0.015.
Values may be sent and summed in bfloat16 or wider, within the bound.
A program may use at most 128 MiB of HBM per device.

```python
import math
import jax
import jax.numpy as jnp
import numpy as np
from jax import lax

D = 2048
INNER_CHANNELS = 8192
N_STATE = 16
FF = 14336
TOPK = 2
L_CH = 128
EXPERTS = 4
SEQUENCE_LENGTH = 512
CAP = 128
N_CTX = 4


def draw_step_size(key, part):
    split_random_keys = jax.random.split(key, 6)
    fast_share = 0.5
    fast_lane = jax.random.bernoulli(split_random_keys[0], fast_share, (INNER_CHANNELS,))
    slow_rate = jnp.exp(jax.random.uniform(split_random_keys[1], (INNER_CHANNELS,), jnp.float32, math.log(0.05), math.log(0.25))) / SEQUENCE_LENGTH
    fast_rate = jnp.exp(jax.random.uniform(split_random_keys[2], (INNER_CHANNELS,), jnp.float32, math.log(1.0 / 50.0), math.log(1.0 / 30.0)))
    baseline_rate = jnp.where(fast_lane, fast_rate, slow_rate)
    jitter_level = jnp.exp(jax.random.uniform(split_random_keys[3], (SEQUENCE_LENGTH, INNER_CHANNELS), jnp.float32, math.log(0.5), math.log(2.0)))
    block_multiplier = jnp.exp(jax.random.uniform(split_random_keys[4], (SEQUENCE_LENGTH // L_CH, INNER_CHANNELS), jnp.float32, math.log(0.5), math.log(2.0)))
    block_multiplier = jnp.repeat(block_multiplier, L_CH, axis=0)
    spike_keys = jax.random.split(split_random_keys[5], 2)
    spike_positions = jax.random.randint(spike_keys[0], (4,), 0, SEQUENCE_LENGTH)
    spike_mask = jnp.zeros((SEQUENCE_LENGTH,), jnp.float32).at[spike_positions].set(1.0)
    spike_length = jnp.exp(jax.random.uniform(spike_keys[1], (INNER_CHANNELS,), jnp.float32, math.log(0.25), math.log(0.7)))
    return baseline_rate[None, :] * jitter_level * block_multiplier + spike_mask[:, None] * spike_length[None, :]


def block_levels(rng, extent, pieces, low, top_value):
    gain, own = 1.0, jax.random.fold_in(rng, 6)
    for position, parts in pieces:
        steps = jnp.exp(jax.random.uniform(jax.random.fold_in(own, position), (parts,), jnp.float32, low / len(pieces), top_value / len(pieces)))
        gain = gain * jnp.repeat(steps, extent[position] // parts).reshape([-1 if axis == position else 1 for axis in range(len(extent))])
    return gain


def shared_out(key, own, number, rows, number_of, top, reach, slope):
    ranking = jax.random.permutation(key, number_of)
    packed, ordinary = portions_of(number_of, rows * top, reach, slope, True), portions_of(number_of, rows * top, reach, slope, False)
    places = jnp.arange(number_of)

    def named(tallies, rotation):
        used = int((tallies > 0).sum())
        fixed = max(1, used // 4)
        shifted = fixed + (places - fixed + rotation * (used - fixed)) % max(1, number_of - fixed)
        return jnp.zeros((number_of,), jnp.int32).at[ranking[jnp.where(places < fixed, places, shifted)]].set(jnp.asarray(tallies, jnp.int32))

    tallies = jnp.where(number % 4 == 0, named(packed, number // 4), named(ordinary, number - number // 4 - 1))
    mixed = jax.random.permutation(jax.random.fold_in(own, 3), number_of)
    donor, receiver = mixed[0:number_of // 2 * 2:2], mixed[1:number_of // 2 * 2:2]
    margin = jnp.minimum(tallies[donor] - 1, reach - tallies[receiver]) // 2
    margin = jnp.where((donor == ranking[0]) | (receiver == ranking[0]) | (tallies[receiver] == 0), 0, jnp.maximum(margin, 0))
    shifted = jax.random.randint(jax.random.fold_in(own, 4), (number_of // 2,), 0, 1 << 20) % (margin + 1)
    tallies = tallies.at[donor].add(-shifted).at[receiver].add(shifted)
    members = jnp.searchsorted(jnp.cumsum(tallies), jnp.arange(rows * top), side="right").astype(jnp.int32)
    grid = members.reshape(top, rows).T
    grid = grid[jax.random.permutation(jax.random.fold_in(own, 1), rows)]
    rotation = jax.random.randint(jax.random.fold_in(own, 2), (rows, 1), 0, top)
    return jnp.take_along_axis(grid, (jnp.arange(top)[None, :] + rotation) % top, axis=1)


def portions_of(count, total, bound, slope, full):
    portions = [(1 << 20) // math.isqrt(grade ** slope) + 1 for grade in range(1, count + 1)]
    largest = bound if full else min(bound, max(-(-total // count), total * portions[0] // sum(portions)))
    least = 1 if total - largest >= count - 1 else 0
    counts, spare = [largest] + [least] * (count - 1), total - largest - least * (count - 1)
    while spare > 0:
        movable = [i for i in range(1, count) if counts[i] < largest] or [i for i in range(1, count) if counts[i] < bound]
        pool, left = sum([portions[i] for i in movable]), spare
        for i in movable:
            addition = min(bound - counts[i], max(1, left * portions[i] // pool), spare)
            counts[i] = counts[i] + addition
            spare = spare - addition
    return np.array(counts)


def noise(own_key, shape, spread, reach, shards=(), kind=jnp.bfloat16):
    drawn = jax.random.normal(own_key, shape, jnp.float32) * spread
    if len(shards) > 0:
        drawn = block_levels(own_key, shape, shards, -0.22, 0.18) * drawn
    return jnp.clip(drawn, min=-reach, max=reach).astype(kind)


def setup_inputs(seed: int = 0) -> dict:
    streams_of = jax.random.split(jax.random.key(seed), 15)
    mamba_in = noise(streams_of[0], (SEQUENCE_LENGTH, INNER_CHANNELS), 1.0, 6.0, ((0, 4), (1, 8)))
    gate_in = noise(streams_of[1], (SEQUENCE_LENGTH, INNER_CHANNELS), 1.0, 6.0, ((0, 4), (1, 8)))
    step_size = draw_step_size(jax.random.fold_in(streams_of[14], 71), 0)
    input_proj = noise(streams_of[3], (N_STATE, SEQUENCE_LENGTH), 1.0, 6.0, ((1, 4),), jnp.float32)
    output_proj = noise(streams_of[4], (N_STATE, SEQUENCE_LENGTH), 1.0, 6.0, ((1, 4),), jnp.float32)
    decay_log = jnp.clip(jax.random.uniform(streams_of[5], (N_STATE, INNER_CHANNELS), jnp.float32, -0.7, 0.7) * block_levels(streams_of[5], (N_STATE, INNER_CHANNELS), ((1, 8),), -0.4, 0.0), -0.7, 0.7)
    skip_gain = jnp.clip(0.5 + 1.5 * jax.random.uniform(streams_of[6], (INNER_CHANNELS,), jnp.float32) ** block_levels(streams_of[6], (INNER_CHANNELS,), ((0, 8),), -0.2, 0.2), 0.5, 2.0)
    out_weight = noise(streams_of[7], (INNER_CHANNELS, D), INNER_CHANNELS ** -0.5, 0.0625, ((0, 8),))
    residual = noise(streams_of[8], (SEQUENCE_LENGTH, D), 1.0, 6.0, ((0, 4), (1, 8)))
    routes_keys = jax.random.split(jax.random.fold_in(streams_of[9], 1), SEQUENCE_LENGTH // L_CH)
    routes_turns = jax.random.permutation(jax.random.fold_in(streams_of[9], 3), SEQUENCE_LENGTH // L_CH)
    routes = jax.vmap(lambda own, number: shared_out(jax.random.fold_in(streams_of[9], 2), own, number, L_CH, EXPERTS, TOPK, CAP, 2))(routes_keys, routes_turns).reshape((SEQUENCE_LENGTH, TOPK))
    norm_gain = jnp.clip(1.0 + 0.15 * jax.random.normal(streams_of[10], (D,), jnp.float32), 0.25, 1.75)
    w_gate = noise(streams_of[11], (EXPERTS, D, FF), D ** -0.5, 0.125, ((0, 4), (2, 8)))
    w_up = noise(streams_of[12], (EXPERTS, D, FF), D ** -0.5, 0.125, ((0, 4), (2, 8)))
    w_down = noise(streams_of[13], (EXPERTS, FF, D), FF ** -0.5, 0.046875, ((0, 4), (1, 4), (2, 2)))
    return {"mamba_in": mamba_in, "gate_in": gate_in, "step_size": step_size, "input_proj": input_proj, "output_proj": output_proj, "decay_log": decay_log, "skip_gain": skip_gain, "out_weight": out_weight, "residual": residual, "routes": routes, "norm_gain": norm_gain, "w_gate": w_gate, "w_up": w_up, "w_down": w_down}


def route_rows(routes, capacity, experts):
    flattened = routes.reshape(-1)
    one_hot = (flattened[:, None] == jnp.arange(experts, dtype=jnp.int32)[None, :]).astype(jnp.int32)
    earlier = jnp.cumsum(one_hot, axis=0) - one_hot
    slot_index = lax.optimization_barrier(jnp.sum(earlier * one_hot, axis=1))
    return (flattened * capacity + slot_index).reshape(routes.shape)

def rms_scale(row_data, norm_gain):
    mean_sq = lax.optimization_barrier(jnp.mean(row_data * row_data, axis=1, keepdims=True))
    return (row_data * lax.rsqrt(mean_sq + 1e-06) * norm_gain).astype(jnp.bfloat16)

def reference(mamba_in, gate_in, step_size, input_proj, output_proj, decay_log, skip_gain, out_weight, residual, routes, norm_gain, w_gate, w_up, w_down):
    decay_rate = -jnp.exp(decay_log)
    signal = mamba_in.astype(jnp.float32)

    def advance(carried, link_item):
        step_row, signal_row, in_row, out_row = link_item
        carried = jnp.exp(step_row[None, :] * decay_rate) * carried + (step_row * signal_row)[None, :] * in_row[:, None]
        return (carried, lax.optimization_barrier(jnp.sum(out_row[:, None] * carried, axis=0)))
    start_state = jnp.zeros((N_STATE, INNER_CHANNELS), jnp.float32)
    unused, readouts = lax.scan(advance, start_state, (step_size, signal, jnp.transpose(input_proj), jnp.transpose(output_proj)))
    gated_out = ((readouts + skip_gain * signal) * jax.nn.silu(gate_in.astype(jnp.float32))).astype(jnp.bfloat16)
    mixed_rows = jnp.dot(gated_out, out_weight, preferred_element_type=jnp.float32) + residual.astype(jnp.float32)
    normed = rms_scale(mixed_rows, norm_gain)
    token_blocks = normed.reshape(N_CTX, L_CH, D)
    route_blocks = routes.reshape(N_CTX, L_CH, TOPK)

    def place(token_rows, block_routes):
        row_ids = route_rows(block_routes, CAP, EXPERTS).reshape(-1)
        copies = jnp.repeat(token_rows, TOPK, axis=0)
        return jnp.zeros((EXPERTS * CAP, D), jnp.bfloat16).at[row_ids].set(copies)
    slots = jax.vmap(place)(token_blocks, route_blocks).reshape(N_CTX, EXPERTS, CAP, D)

    def run_expert(expert_item):
        expert_rows, gate_w, up_w, down_w = expert_item
        flat_rows = expert_rows.reshape(N_CTX * CAP, D)
        gate_part = jnp.dot(flat_rows, gate_w, preferred_element_type=jnp.float32)
        up_part = jnp.dot(flat_rows, up_w, preferred_element_type=jnp.float32)
        hidden = (jax.nn.silu(gate_part) * up_part).astype(jnp.bfloat16)
        result = jnp.dot(hidden, down_w, preferred_element_type=jnp.float32).astype(jnp.bfloat16)
        return result.reshape(N_CTX, CAP, D)
    outputs = lax.map(run_expert, (jnp.transpose(slots, (1, 0, 2, 3)), w_gate, w_up, w_down))
    return jnp.transpose(outputs, (1, 0, 2, 3))
```

```python
import math

import jax
import jax.numpy as jnp
from jax import lax
from jax.experimental import pallas as pl
from jax.experimental.pallas import tpu as pltpu
from jax.sharding import PartitionSpec as P

MESH = pl.DeviceIdType.MESH
LOG2E = math.log2(math.e)
CHUNKS = 4
TILE = 256


def prefix_2(value, axis, join, neutral):
    count, mine = (lax.axis_size(axis), lax.axis_index(axis))
    pieces = jax.tree.map(lambda part: lax.all_gather(part, axis), value)
    so_far = jax.tree.map(
        lambda part, zero: jnp.full_like(part, 0) + jnp.asarray(zero, part.dtype), value, neutral
    )

    def step(position, so_far):
        longer = join(so_far, jax.tree.map(lambda part: part[position], pieces))
        return jax.tree.map(lambda new, old: jnp.where(position < mine, new, old), longer, so_far)

    return lax.fori_loop(0, count - 1, step, so_far)


def route_rows(routes, capacity, experts):
    flattened = routes.reshape(-1)
    one_hot = (flattened[:, None] == jnp.arange(experts, dtype=jnp.int32)[None, :]).astype(
        jnp.float32
    )
    pairs = jnp.arange(flattened.shape[0], dtype=jnp.int32)
    before = (pairs[None, :] < pairs[:, None]).astype(jnp.float32)
    earlier = jnp.dot(before, one_hot, preferred_element_type=jnp.float32)
    slot_index = jnp.sum(earlier * one_hot, axis=1).astype(jnp.int32)
    return (flattened * capacity + slot_index).reshape(routes.shape)


def pick_rows(row_ids, first_row, row_count):
    targets = first_row + jnp.arange(row_count, dtype=jnp.int32)
    matches = row_ids[None, :, :] == targets[:, None, None]
    return jnp.sum(matches.astype(jnp.float32), axis=2).astype(jnp.bfloat16)


def rms_scale(row_data, norm_gain):
    mean_sq = jnp.mean(row_data * row_data, axis=1, keepdims=True)
    return (row_data * lax.rsqrt(mean_sq + 1e-06) * norm_gain).astype(jnp.bfloat16)


def combine_link(earlier, later_link):
    return (earlier[0] * later_link[0], later_link[0] * earlier[1] + later_link[1])


def fits(mamba_in, out_weight, residual, w_gate, w_down, capacity):
    length, channels = mamba_in.shape
    depth = out_weight.shape[1]
    experts = lax.axis_size("exp")
    return (
        lax.axis_size("tp") == 2
        and lax.axis_size("ctx") == 4
        and experts == 4
        and channels % 128 == 0
        and channels // 128 <= 8
        and capacity == length
        and length % 128 == 0
        and depth % (2 * experts * 128) == 0
        and w_gate.shape[2] % TILE == 0
        and w_down.shape[0] == 1
    )


def fused_kernel(
    mamba_hbm, gate_hbm, step_hbm, in_ref, read_ref, decay_ref, skip_ref, mix_hbm,
    residual_ref, gain_ref, wg_hbm, wu_hbm, wd_hbm, out_ref,
    step_v, mamba_v, gate_v, drive_v, rate_v, spread_v, select_v, history, state_v,
    ends, totals, mix_v, wg, wu, wd,
    mixed, z_inbox, y_outbox, y_inbox, tokens, scale_v, own, other, acc, part, inbox,
    load_sem, g_sem, u_sem, e_send, e_recv, t_send, t_recv, z_send, z_recv, y_send, y_recv,
    a_send, a_recv, c_send, c_recv, h_send, h_recv, r_send, r_recv,
):
    ctx, exp, tp = lax.axis_index("ctx"), lax.axis_index("exp"), lax.axis_index("tp")
    experts = lax.axis_size("exp")
    blocks = lax.axis_size("ctx")
    length, channels = step_v.shape
    states = rate_v.shape[0]
    piece = length // CHUNKS
    lanes = channels // 128
    span = tokens.shape[-1]
    depth = span * experts
    tiles = wg.shape[0]
    bf16, f32 = jnp.bfloat16, jnp.float32

    ctx_peers = (ctx + 1 - 2 * lax.rem(ctx, 2), lax.rem(ctx + 2, blocks), blocks - 1 - ctx)
    z_peers = [lax.rem(exp + d, experts) for d in range(1, experts)]

    barrier = pltpu.get_barrier_semaphore()
    greeted = (
        [{"tp": 1 - tp}] + [{"exp": z} for z in z_peers] + [{"ctx": c} for c in ctx_peers]
    )
    for device in greeted:
        pl.semaphore_signal(barrier, inc=1, device_id=device, device_id_type=MESH)

    def remote(src, dst, send_sem, recv_sem, device):
        return pltpu.make_async_remote_copy(
            src_ref=src, dst_ref=dst, send_sem=send_sem, recv_sem=recv_sem,
            device_id=device, device_id_type=MESH,
        )

    step_copy = pltpu.make_async_copy(step_hbm, step_v, load_sem.at[0])
    mamba_copy = pltpu.make_async_copy(mamba_hbm, mamba_v, load_sem.at[1])
    gate_copy = pltpu.make_async_copy(gate_hbm, gate_v, load_sem.at[2])
    mix_copy = pltpu.make_async_copy(mix_hbm, mix_v, load_sem.at[3])
    wd_copy = pltpu.make_async_copy(wd_hbm.at[0], wd, load_sem.at[4])

    def columns(k):
        return pl.ds(pl.multiple_of(k * TILE, TILE), TILE)

    def wg_copy(k):
        return pltpu.make_async_copy(wg_hbm.at[0, :, columns(k)], wg.at[k], g_sem.at[k])

    def wu_copy(k):
        return pltpu.make_async_copy(wu_hbm.at[0, :, columns(k)], wu.at[k], u_sem.at[k])

    for copy in (step_copy, mamba_copy, gate_copy, mix_copy):
        copy.start()
    for k in range(tiles):
        wg_copy(k).start()
        wu_copy(k).start()
    wd_copy.start()

    rate_v[...] = -jnp.exp(decay_ref[...]) * LOG2E
    for t in range(length):
        spread_v[t] = jnp.broadcast_to(in_ref[:, t : t + 1], (states, 128))
    step_copy.wait()
    mamba_copy.wait()
    drive_v[...] = mamba_v[...].astype(f32) * step_v[...]

    def lane(j):
        return slice(j * 128, (j + 1) * 128)

    def advance(first, count, carried, keep):
        rates = [rate_v[:, lane(j)] for j in range(lanes)]

        def eight(g, carried):
            carried = list(carried)
            base = pl.multiple_of(first + g * 8, 8)
            steps = [step_v[pl.ds(base, 8), lane(j)] for j in range(lanes)]
            drives = [drive_v[pl.ds(base, 8), lane(j)] for j in range(lanes)]
            for i in range(8):
                spread = spread_v[base + i]
                for j in range(lanes):
                    step = jnp.broadcast_to(steps[j][i : i + 1], (states, 128))
                    drive = jnp.broadcast_to(drives[j][i : i + 1], (states, 128))
                    carried[j] = jnp.exp2(step * rates[j]) * carried[j] + drive * spread
                    if keep:
                        row = pl.multiple_of((g * 8 + i) * states, states)
                        history[pl.ds(row, states), lane(j)] = carried[j].astype(bf16)
            return tuple(carried)

        return lax.fori_loop(0, count // 8, eight, tuple(carried))

    local = advance(0, length, (jnp.zeros((states, 128), f32),) * lanes, False)
    sums = jnp.sum(step_v[...], axis=0, keepdims=True)
    for j in range(lanes):
        ends[ctx, :, lane(j)] = local[j].astype(bf16)
        totals[ctx, j : j + 1, :] = sums[:, lane(j)]

    pl.semaphore_wait(barrier, len(greeted))
    end_copies = []
    for n, peer in enumerate(ctx_peers):
        end_copies.append(
            remote(ends.at[ctx], ends.at[ctx], e_send.at[n], e_recv.at[n], {"ctx": peer})
        )
        end_copies.append(
            remote(totals.at[ctx], totals.at[ctx], t_send.at[n], t_recv.at[n], {"ctx": peer})
        )
    for copy in end_copies:
        copy.start()

    shape = (length, piece * states)
    column = lax.broadcasted_iota(jnp.int32, (states, piece * states), 1)
    row = lax.broadcasted_iota(jnp.int32, (states, piece * states), 0)
    repeat = jnp.where(lax.rem(column, states) == row, 1.0, 0.0).astype(bf16)
    wide = lax.dot_general(
        read_ref[...].astype(bf16), repeat, (((0,), (0,)), ((), ())), preferred_element_type=f32
    )
    position = lax.rem(lax.broadcasted_iota(jnp.int32, shape, 0), piece)
    owner = lax.broadcasted_iota(jnp.int32, shape, 1) // states
    select_v[...] = jnp.where(position == owner, wide, 0.0).astype(bf16)

    for copy in end_copies:
        copy.wait_recv()
    for j in range(lanes):
        rate = rate_v[:, lane(j)]
        incoming = jnp.zeros((states, 128), f32)
        for b in range(blocks - 1):
            total = jnp.broadcast_to(totals[b, j : j + 1, :], (states, 128))
            longer = jnp.exp2(total * rate) * incoming + ends[b, :, lane(j)].astype(f32)
            incoming = jnp.where(b < ctx, longer, incoming)
        state_v[:, lane(j)] = incoming

    gate_copy.wait()
    mix_copy.wait()

    def mix(r):
        carried = advance(r * piece, piece, [state_v[:, lane(j)] for j in range(lanes)], True)
        for j in range(lanes):
            state_v[:, lane(j)] = carried[j]
        rows = slice(r * piece, (r + 1) * piece)
        readout = jnp.dot(select_v[rows, :], history[...], preferred_element_type=f32)
        gate = gate_v[rows, :].astype(f32)
        signal = mamba_v[rows, :].astype(f32)
        gated = (readout + skip_ref[...] * signal) * (gate / (1.0 + jnp.exp(-gate)))
        gated = gated.astype(bf16)
        for z in range(experts):
            mixed[r, z] = jnp.dot(
                gated, mix_v[:, z * span : (z + 1) * span], preferred_element_type=f32
            ).astype(bf16)

    def z_copy(r, d):
        peer = z_peers[d - 1]
        return remote(
            mixed.at[r, peer], z_inbox.at[r, d - 1], z_send.at[r, d - 1], z_recv.at[r, d - 1],
            {"exp": peer},
        )

    def y_copy(r):
        return remote(
            y_outbox.at[r], y_inbox.at[r], y_send.at[r], y_recv.at[r], {"tp": 1 - tp}
        )

    def a_copy(r, d):
        here = tokens.at[r, exp, ctx]
        return remote(here, here, a_send.at[r, d - 1], a_recv.at[r, d - 1], {"exp": z_peers[d - 1]})

    def c_copy(r, d, n):
        here = tokens.at[r, lax.rem(exp - d + experts, experts), ctx]
        return remote(here, here, c_send.at[r, d, n], c_recv.at[r, d, n], {"ctx": ctx_peers[n]})

    def scatter(r):
        for d in (2, 1, 3):
            z_copy(r, d).start()

    def swap(r):
        rows = slice(r * piece, (r + 1) * piece)
        lifted = residual_ref[rows, :].astype(f32)
        total = jnp.concatenate(
            [jnp.where(tp == n, lifted, 0.0) for n in range(2)], axis=1
        ) + mixed[r, exp].astype(f32)
        for d in range(1, experts):
            z_copy(r, d).wait_recv()
            total = total + z_inbox[r, d - 1].astype(f32)
        y_outbox[r] = total.astype(bf16)
        y_copy(r).start()

    def gather(r):
        y_copy(r).wait_recv()
        total = y_outbox[r].astype(f32) + y_inbox[r].astype(f32)
        gain = gain_ref[:, pl.ds(pl.multiple_of(exp * span, span), span)]
        tokens[r, exp, ctx] = (total * gain).astype(bf16)
        for d in (2, 1, 3):
            a_copy(r, d).start()
        for n in range(blocks - 1):
            c_copy(r, 0, n).start()

    def share(r):
        for d in range(1, experts):
            a_copy(r, d).wait_recv()
            for n in range(blocks - 1):
                c_copy(r, d, n).start()

    def arrived(r, kinds):
        for n in kinds:
            for d in range(experts):
                c_copy(r, d, n).wait_recv()

    near = pl.multiple_of(ctx // 2 * 2, 2)
    passes = [(0, near, 2), (0, 2 - near, 2)] + [(r, 0, blocks) for r in range(1, CHUNKS)]

    def pass_rows(p):
        r, first, count = passes[p]
        return pl.ds(pl.multiple_of(first * piece, piece), count * piece)

    def pass_tokens(p, z):
        r, first, count = passes[p]
        return tokens[r, z, pl.ds(first, count)].reshape(count * piece, span)

    def hidden_copy(p, k):
        r = passes[p][0]
        return remote(
            own.at[r, k, pass_rows(p)], other.at[r, k, pass_rows(p)],
            h_send.at[p, k], h_recv.at[p, k], {"tp": 1 - tp},
        )

    def measure(p):
        count = passes[p][2] * piece
        squares = jnp.zeros((count, 1), f32)
        for z in range(experts):
            inverse = 1.0 / gain_ref[:, z * span : (z + 1) * span]
            plain = pass_tokens(p, z).astype(f32) * inverse
            squares = squares + jnp.sum(plain * plain, axis=1, keepdims=True)
        scale = lax.rsqrt(squares / depth + 1e-06)
        scale_v[:count, :] = jnp.broadcast_to(scale, (count, 128))

    def hidden(p, low, high):
        r, _, count = passes[p]
        rows_here = count * piece

        def one(k, unused):
            if p == 0:
                wg_copy(k).wait()
                wu_copy(k).wait()
            rows = jnp.concatenate([pass_tokens(p, z) for z in range(experts)], axis=1)
            scale = jnp.concatenate([scale_v[:rows_here, :]] * (TILE // 128), axis=1)
            gate = jnp.dot(rows, wg[k], preferred_element_type=f32) * scale
            up = jnp.dot(rows, wu[k], preferred_element_type=f32) * scale
            own[r, k, pass_rows(p), :] = (gate / (1.0 + jnp.exp(-gate)) * up).astype(bf16)
            hidden_copy(p, k).start()
            return unused

        lax.fori_loop(low, high, one, 0)

    def down_rows(half, k):
        return pl.ds(pl.multiple_of((half * tiles + k) * TILE, TILE), TILE)

    def down_own(r):
        acc[r] = jnp.zeros(acc.shape[1:], f32)

        def one(k, unused):
            acc[r] += jnp.dot(own[r, k], wd[down_rows(tp, k), :], preferred_element_type=f32)
            return unused

        lax.fori_loop(0, tiles, one, 0)

    def part_copy(r, n):
        peer = ctx_peers[n]
        return remote(
            part.at[r, peer], inbox.at[r, n], r_send.at[r, n], r_recv.at[r, n], {"ctx": peer}
        )

    def down_other(r):
        here = [p for p in range(len(passes)) if passes[p][0] == r]

        def one(k, unused):
            for p in here:
                hidden_copy(p, k).wait_recv()
            acc[r] += jnp.dot(
                other[r, k], wd[down_rows(1 - tp, k), :], preferred_element_type=f32
            )
            return unused

        lax.fori_loop(0, tiles, one, 0)
        part[r] = acc[r].astype(bf16).reshape(part.shape[1:])
        for n in range(blocks - 1):
            part_copy(r, n).start()

    def finish(r):
        total = acc[r, pl.ds(pl.multiple_of(ctx * piece, piece), piece), :]
        for n in range(blocks - 1):
            part_copy(r, n).wait_recv()
            total = total + inbox[r, n].astype(f32)
        out_ref[r * piece : (r + 1) * piece, :] = total.astype(out_ref.dtype)

    half = (tiles + 1) // 2
    mix(0)
    scatter(0)
    mix(1)
    scatter(1)
    mix(2)
    swap(0)
    mix(3)
    gather(0)
    scatter(2)
    swap(1)
    share(0)
    arrived(0, (0,))
    measure(0)
    hidden(0, 0, half)
    gather(1)
    scatter(3)
    swap(2)
    hidden(0, half, tiles)
    arrived(0, (1, 2))
    measure(1)
    hidden(1, 0, half)
    share(1)
    gather(2)
    hidden(1, half, tiles)
    swap(3)
    arrived(1, (0, 1, 2))
    measure(2)
    hidden(2, 0, half)
    share(2)
    gather(3)
    hidden(2, half, tiles)
    wd_copy.wait()
    down_own(0)
    share(3)
    arrived(2, (0, 1, 2))
    measure(3)
    hidden(3, 0, tiles)
    down_own(1)
    arrived(3, (0, 1, 2))
    measure(4)
    hidden(4, 0, tiles)
    down_other(0)
    down_own(2)
    down_own(3)
    finish(0)
    down_other(1)
    finish(1)
    down_other(2)
    finish(2)
    down_other(3)
    finish(3)

    for copy in end_copies:
        copy.wait_send()
    for r in range(CHUNKS):
        y_copy(r).wait_send()
        for d in range(1, experts):
            z_copy(r, d).wait_send()
            a_copy(r, d).wait_send()
        for n in range(blocks - 1):
            part_copy(r, n).wait_send()
            for d in range(experts):
                c_copy(r, d, n).wait_send()

    def drain(k, unused):
        for p in range(len(passes)):
            hidden_copy(p, k).wait_send()
        return unused

    lax.fori_loop(0, tiles, drain, 0)


def fused(
    mamba_in, gate_in, step_size, input_proj, output_proj, decay_log, skip_gain,
    out_weight, residual, norm_gain, w_gate, w_up, w_down,
):
    length, channels = mamba_in.shape
    states = decay_log.shape[0]
    depth = out_weight.shape[1]
    experts, blocks = lax.axis_size("exp"), lax.axis_size("ctx")
    hidden, width = w_gate.shape[2], w_down.shape[2]
    piece, span, tiles = length // CHUNKS, depth // experts, hidden // TILE
    bf16, f32, dma = jnp.bfloat16, jnp.float32, pltpu.SemaphoreType.DMA
    vmem, anywhere = pl.BlockSpec(memory_space=pltpu.VMEM), pl.BlockSpec(memory_space=pl.ANY)
    passes = CHUNKS + 1
    scratch = [
        pltpu.VMEM((length, channels), f32),
        pltpu.VMEM((length, channels), bf16),
        pltpu.VMEM((length, channels), bf16),
        pltpu.VMEM((length, channels), f32),
        pltpu.VMEM((states, channels), f32),
        pltpu.VMEM((length, states, 128), f32),
        pltpu.VMEM((length, piece * states), bf16),
        pltpu.VMEM((piece * states, channels), bf16),
        pltpu.VMEM((states, channels), f32),
        pltpu.VMEM((blocks, states, channels), bf16),
        pltpu.VMEM((blocks, 8, 128), f32),
        pltpu.VMEM((channels, depth), bf16),
        pltpu.VMEM((tiles, depth, TILE), bf16),
        pltpu.VMEM((tiles, depth, TILE), bf16),
        pltpu.VMEM((2 * hidden, width), bf16),
        pltpu.VMEM((CHUNKS, experts, piece, span), bf16),
        pltpu.VMEM((CHUNKS, experts - 1, piece, span), bf16),
        pltpu.VMEM((CHUNKS, piece, span), bf16),
        pltpu.VMEM((CHUNKS, piece, span), bf16),
        pltpu.VMEM((CHUNKS, experts, blocks, piece, span), bf16),
        pltpu.VMEM((blocks * piece, 128), f32),
        pltpu.VMEM((CHUNKS, tiles, blocks * piece, TILE), bf16),
        pltpu.VMEM((CHUNKS, tiles, blocks * piece, TILE), bf16),
        pltpu.VMEM((CHUNKS, blocks * piece, width), f32),
        pltpu.VMEM((CHUNKS, blocks, piece, width), bf16),
        pltpu.VMEM((CHUNKS, blocks - 1, piece, width), bf16),
        dma((5,)),
        dma((tiles,)),
        dma((tiles,)),
        dma((blocks - 1,)),
        dma((blocks - 1,)),
        dma((blocks - 1,)),
        dma((blocks - 1,)),
        dma((CHUNKS, experts - 1)),
        dma((CHUNKS, experts - 1)),
        dma((CHUNKS,)),
        dma((CHUNKS,)),
        dma((CHUNKS, experts - 1)),
        dma((CHUNKS, experts - 1)),
        dma((CHUNKS, experts, blocks - 1)),
        dma((CHUNKS, experts, blocks - 1)),
        dma((passes, tiles)),
        dma((passes, tiles)),
        dma((CHUNKS, blocks - 1)),
        dma((CHUNKS, blocks - 1)),
    ]
    return pl.pallas_call(
        fused_kernel,
        out_shape=jax.ShapeDtypeStruct((length, width), bf16),
        in_specs=[anywhere] * 3 + [vmem] * 4 + [anywhere] + [vmem] * 2 + [anywhere] * 3,
        out_specs=vmem,
        scratch_shapes=scratch,
        compiler_params=pltpu.CompilerParams(
            collective_id=0, has_side_effects=True, vmem_limit_bytes=60 << 20
        ),
        name="fused",
    )(
        mamba_in, gate_in, step_size, input_proj, output_proj, decay_log, skip_gain[None, :],
        out_weight, residual, norm_gain[None, :], w_gate, w_up, w_down,
    )


def place_kernel(rows_ref, routes_ref, out_ref):
    mine = lax.axis_index("exp")
    length = rows_ref.shape[0]
    routes = routes_ref[...]
    shape = (length, length)
    named = jnp.zeros((length, 1), jnp.float32)
    for k in range(routes.shape[1]):
        named = named + jnp.where(routes[:, k : k + 1] == mine, 1.0, 0.0)
    named = jnp.broadcast_to(named, shape)
    row = lax.broadcasted_iota(jnp.int32, shape, 0)
    column = lax.broadcasted_iota(jnp.int32, shape, 1)
    before = jnp.where(column < row, 1.0, 0.0).astype(jnp.bfloat16)
    slot = jnp.dot(before, named.astype(jnp.bfloat16), preferred_element_type=jnp.float32)
    pick = jnp.where(slot == column.astype(jnp.float32), named, 0.0).astype(jnp.bfloat16)
    out_ref[...] = lax.dot_general(
        pick, rows_ref[...], (((0,), (0,)), ((), ())), preferred_element_type=jnp.float32
    ).astype(out_ref.dtype)


def placed_rows(rows, routes):
    vmem = pl.BlockSpec(memory_space=pltpu.VMEM)
    return pl.pallas_call(
        place_kernel,
        out_shape=jax.ShapeDtypeStruct(rows.shape, rows.dtype),
        in_specs=[vmem] * 2,
        out_specs=vmem,
        name="place",
    )(rows, routes)


def scanned_small(mamba_in, gate_in, step_size, input_proj, output_proj, decay_log, skip_gain):
    decay_rate = -jnp.exp(decay_log)
    signal = mamba_in.astype(jnp.float32)
    decays = jnp.exp(step_size[:, None, :] * decay_rate[None, :, :])
    driving = (step_size * signal)[:, None, :] * jnp.transpose(input_proj)[:, :, None]
    cum_decay, local_state = lax.associative_scan(combine_link, (decays, driving), axis=0)
    summary = (cum_decay[-1], local_state[-1])
    identity = (jnp.ones_like(summary[0]), jnp.zeros_like(summary[1]))
    prefix = prefix_2(summary, "ctx", combine_link, identity)
    incoming = prefix[1]
    full_state = local_state + cum_decay * incoming[None, :, :]
    readout = jnp.sum(jnp.transpose(output_proj)[:, :, None] * full_state, axis=1)
    return ((readout + skip_gain * signal) * jax.nn.silu(gate_in.astype(jnp.float32))).astype(
        jnp.bfloat16
    )


def body(
    mamba_in,
    gate_in,
    step_size,
    input_proj,
    output_proj,
    decay_log,
    skip_gain,
    out_weight,
    residual,
    routes,
    norm_gain,
    w_gate,
    w_up,
    w_down,
):
    length = mamba_in.shape[0]
    experts = lax.axis_size("exp")
    top_count = routes.shape[1]
    capacity = length * top_count * 2 // experts
    if fits(mamba_in, out_weight, residual, w_gate, w_down, capacity):
        total = fused(
            mamba_in, gate_in, step_size, input_proj, output_proj, decay_log, skip_gain,
            out_weight, residual, norm_gain, w_gate, w_up, w_down,
        )
        return placed_rows(total, routes)[None, None]
    gated_out = scanned_small(
        mamba_in, gate_in, step_size, input_proj, output_proj, decay_log, skip_gain
    )
    row_ids = route_rows(routes, capacity, experts)
    rows_here = capacity // lax.axis_size("tp")
    col_width = residual.shape[1]
    model_width = out_weight.shape[1]
    offset = lax.axis_index(("exp", "tp")) * col_width
    mixed_rows = jnp.dot(gated_out, out_weight, preferred_element_type=jnp.float32)
    lifted = residual.astype(jnp.float32)
    placed = jnp.zeros((lifted.shape[0], model_width), jnp.float32)
    token_part = lax.psum_scatter(
        mixed_rows + lax.dynamic_update_slice_in_dim(placed, lifted, offset, 1),
        ("exp", "tp"),
        scatter_dimension=0,
        tiled=True,
    )
    every_token = lax.all_gather(
        rms_scale(token_part, norm_gain), ("exp", "tp"), axis=0, tiled=True
    )
    picker = pick_rows(row_ids, lax.axis_index(("exp", "tp")) * rows_here, rows_here)
    normed = jnp.dot(picker, every_token, preferred_element_type=jnp.float32).astype(jnp.bfloat16)
    row_block = lax.all_gather(normed, ("ctx", "tp"), axis=0, tiled=True)
    gate_part = jnp.dot(row_block, w_gate[0], preferred_element_type=jnp.float32)
    up_part = jnp.dot(row_block, w_up[0], preferred_element_type=jnp.float32)
    hidden = (jax.nn.silu(gate_part) * up_part).astype(jnp.bfloat16)
    local_down = w_down[0]
    partial_out = jnp.dot(
        lax.all_gather(hidden, "tp", axis=1, tiled=True),
        local_down,
        preferred_element_type=jnp.float32,
    )
    result = lax.psum_scatter(
        partial_out.astype(jnp.bfloat16), "ctx", scatter_dimension=0, tiled=True
    )
    return result[None, None]


def solution(mesh):
    in_specs = (
        P("ctx", ("exp", "tp")),
        P("ctx", ("exp", "tp")),
        P("ctx", ("exp", "tp")),
        P(None, "ctx"),
        P(None, "ctx"),
        P(None, ("exp", "tp")),
        P(("exp", "tp")),
        P(("exp", "tp"), None),
        P("ctx", ("exp", "tp")),
        P("ctx", None),
        P(),
        P("exp", None, ("ctx", "tp")),
        P("exp", None, ("ctx", "tp")),
        P("exp", "ctx", "tp"),
    )
    out_specs = P("ctx", "exp", None, "tp")
    return jax.shard_map(body, mesh=mesh, in_specs=in_specs, out_specs=out_specs, check_vma=False)
```

```python
import math

import jax
import jax.numpy as jnp
from jax import lax
from jax.experimental import pallas as pl
from jax.experimental.pallas import tpu as pltpu
from jax.sharding import PartitionSpec as P

MESH = pl.DeviceIdType.MESH
LOG2E = math.log2(math.e)
CHUNKS = (2, 2, 2, 2)
TILE = 256


def prefix_2(value, axis, join, neutral):
    count, mine = (lax.axis_size(axis), lax.axis_index(axis))
    pieces = jax.tree.map(lambda part: lax.all_gather(part, axis), value)
    so_far = jax.tree.map(
        lambda part, zero: jnp.full_like(part, 0) + jnp.asarray(zero, part.dtype), value, neutral
    )

    def step(position, so_far):
        longer = join(so_far, jax.tree.map(lambda part: part[position], pieces))
        return jax.tree.map(lambda new, old: jnp.where(position < mine, new, old), longer, so_far)

    return lax.fori_loop(0, count - 1, step, so_far)


def route_rows(routes, capacity, experts):
    flattened = routes.reshape(-1)
    one_hot = (flattened[:, None] == jnp.arange(experts, dtype=jnp.int32)[None, :]).astype(
        jnp.float32
    )
    pairs = jnp.arange(flattened.shape[0], dtype=jnp.int32)
    before = (pairs[None, :] < pairs[:, None]).astype(jnp.float32)
    earlier = jnp.dot(before, one_hot, preferred_element_type=jnp.float32)
    slot_index = jnp.sum(earlier * one_hot, axis=1).astype(jnp.int32)
    return (flattened * capacity + slot_index).reshape(routes.shape)


def pick_rows(row_ids, first_row, row_count):
    targets = first_row + jnp.arange(row_count, dtype=jnp.int32)
    matches = row_ids[None, :, :] == targets[:, None, None]
    return jnp.sum(matches.astype(jnp.float32), axis=2).astype(jnp.bfloat16)


def rms_scale(row_data, norm_gain):
    mean_sq = jnp.mean(row_data * row_data, axis=1, keepdims=True)
    return (row_data * lax.rsqrt(mean_sq + 1e-06) * norm_gain).astype(jnp.bfloat16)


def combine_link(earlier, later_link):
    return (earlier[0] * later_link[0], later_link[0] * earlier[1] + later_link[1])


def fits(mamba_in, out_weight, residual, w_gate, w_down, capacity):
    length, channels = mamba_in.shape
    depth = out_weight.shape[1]
    experts = lax.axis_size("exp")
    return (
        lax.axis_size("tp") == 2
        and lax.axis_size("ctx") == 4
        and experts == 4
        and channels % 128 == 0
        and channels // 128 <= 8
        and capacity == length
        and length % 128 == 0
        and depth % (2 * experts * 128) == 0
        and w_gate.shape[2] % TILE == 0
        and w_down.shape[0] == 1
    )


def chunk_sizes(length):
    part = length // 8
    return tuple(n * part for n in CHUNKS)


def hidden_passes(chunks):
    return [((0,), 0), ((0,), 1)] + [((r,), 2) for r in range(1, chunks)]


def fused_kernel(
    mamba_hbm, gate_hbm, step_hbm, in_ref, read_ref, decay_ref, skip_ref, mix_hbm,
    residual_ref, gain_ref, wg_hbm, wu_hbm, wd_hbm, out_ref,
    step_v, mamba_v, gate_v, drive_v, rate_v, spread_v, select_v, history, state_v,
    ends, totals, mix_v, wg, wu, wd,
    scale_v, direct, direct_inbox, mixed, z_inbox, y_outbox, y_inbox, tokens, own, other, acc,
    part, inbox,
    load_sem, g_sem, u_sem, e_send, e_recv, t_send, t_recv, d_send, d_recv, b_send, b_recv,
    z_send, z_recv, y_send, y_recv, a_send, a_recv, c_send, c_recv, h_send, h_recv,
    r_send, r_recv,
):
    ctx, exp, tp = lax.axis_index("ctx"), lax.axis_index("exp"), lax.axis_index("tp")
    experts = lax.axis_size("exp")
    blocks = lax.axis_size("ctx")
    length, channels = step_v.shape
    states = rate_v.shape[0]
    sizes = chunk_sizes(length)
    starts = [sum(sizes[:r]) for r in range(len(sizes))]
    chunks = len(sizes)
    longest = max(sizes)
    lanes = channels // 128
    span = tokens[-1].shape[-1]
    width = span // 2
    depth = span * experts
    tiles = wg.shape[0]
    bf16, f32 = jnp.bfloat16, jnp.float32

    ctx_peers = (ctx + 1 - 2 * lax.rem(ctx, 2), lax.rem(ctx + 2, blocks), blocks - 1 - ctx)
    z_peers = [lax.rem(exp + d, experts) for d in range(1, experts)]

    barrier = pltpu.get_barrier_semaphore()
    place, places = exp * 2 + tp, 2 * experts

    def member(d):
        peer = lax.rem(place + d, places)
        return peer, {"exp": peer // 2, "tp": lax.rem(peer, 2)}

    greeted = [member(d)[1] for d in range(1, places)] + [{"ctx": c} for c in ctx_peers]
    for device in greeted:
        pl.semaphore_signal(barrier, inc=1, device_id=device, device_id_type=MESH)

    def remote(src, dst, send_sem, recv_sem, device):
        return pltpu.make_async_remote_copy(
            src_ref=src, dst_ref=dst, send_sem=send_sem, recv_sem=recv_sem,
            device_id=device, device_id_type=MESH,
        )

    step_copy = pltpu.make_async_copy(step_hbm, step_v, load_sem.at[0])
    mamba_copy = pltpu.make_async_copy(mamba_hbm, mamba_v, load_sem.at[1])
    gate_copy = pltpu.make_async_copy(gate_hbm, gate_v, load_sem.at[2])
    mix_copy = pltpu.make_async_copy(mix_hbm, mix_v, load_sem.at[3])
    wd_copy = pltpu.make_async_copy(wd_hbm.at[0], wd, load_sem.at[4])

    def columns(k):
        return pl.ds(pl.multiple_of(k * TILE, TILE), TILE)

    def wg_copy(k):
        return pltpu.make_async_copy(wg_hbm.at[0, :, columns(k)], wg.at[k], g_sem.at[k])

    def wu_copy(k):
        return pltpu.make_async_copy(wu_hbm.at[0, :, columns(k)], wu.at[k], u_sem.at[k])

    step_copy.start()
    mamba_copy.start()

    rate_v[...] = -jnp.exp(decay_ref[...]) * LOG2E
    for t in range(length):
        spread_v[t] = jnp.broadcast_to(in_ref[:, t : t + 1], (states, 128))
    step_copy.wait()
    mamba_copy.wait()
    gate_copy.start()
    mix_copy.start()
    drive_v[...] = mamba_v[...].astype(f32) * step_v[...]

    def lane(j):
        return slice(j * 128, (j + 1) * 128)

    def advance(first, count, carried, keep):
        rates = [rate_v[:, lane(j)] for j in range(lanes)]

        def eight(g, carried):
            carried = list(carried)
            base = pl.multiple_of(first + g * 8, 8)
            steps = [step_v[pl.ds(base, 8), lane(j)] for j in range(lanes)]
            drives = [drive_v[pl.ds(base, 8), lane(j)] for j in range(lanes)]
            for i in range(8):
                spread = spread_v[base + i]
                for j in range(lanes):
                    step = jnp.broadcast_to(steps[j][i : i + 1], (states, 128))
                    drive = jnp.broadcast_to(drives[j][i : i + 1], (states, 128))
                    carried[j] = jnp.exp2(step * rates[j]) * carried[j] + drive * spread
                    if keep:
                        row = pl.multiple_of((g * 8 + i) * states, states)
                        history[pl.ds(row, states), lane(j)] = carried[j].astype(bf16)
            return tuple(carried)

        return lax.fori_loop(0, count // 8, eight, tuple(carried))

    local = advance(0, length, (jnp.zeros((states, 128), f32),) * lanes, False)
    sums = jnp.sum(step_v[...], axis=0, keepdims=True)
    for j in range(lanes):
        ends[ctx, :, lane(j)] = local[j].astype(bf16)
        totals[ctx, j : j + 1, :] = sums[:, lane(j)]

    pl.semaphore_wait(barrier, len(greeted))
    end_copies = []
    for n, peer in enumerate(ctx_peers):
        end_copies.append(
            remote(ends.at[ctx], ends.at[ctx], e_send.at[n], e_recv.at[n], {"ctx": peer})
        )
        end_copies.append(
            remote(totals.at[ctx], totals.at[ctx], t_send.at[n], t_recv.at[n], {"ctx": peer})
        )
    for copy in end_copies:
        copy.start()
    for k in range(tiles):
        wg_copy(k).start()
        wu_copy(k).start()

    column = lax.broadcasted_iota(jnp.int32, (states, longest * states), 1)
    row = lax.broadcasted_iota(jnp.int32, (states, longest * states), 0)
    repeat = jnp.where(lax.rem(column, states) == row, 1.0, 0.0).astype(bf16)
    wide = lax.dot_general(
        read_ref[...].astype(bf16), repeat, (((0,), (0,)), ((), ())), preferred_element_type=f32
    )
    for r in range(chunks):
        shape = (sizes[r], longest * states)
        position = lax.broadcasted_iota(jnp.int32, shape, 0)
        owner = lax.broadcasted_iota(jnp.int32, shape, 1) // states
        rows = slice(starts[r], starts[r] + sizes[r])
        select_v[rows, :] = jnp.where(position == owner, wide[rows, :], 0.0).astype(bf16)

    for copy in end_copies:
        copy.wait_recv()
    for j in range(lanes):
        rate = rate_v[:, lane(j)]
        incoming = jnp.zeros((states, 128), f32)
        for b in range(blocks - 1):
            total = jnp.broadcast_to(totals[b, j : j + 1, :], (states, 128))
            longer = jnp.exp2(total * rate) * incoming + ends[b, :, lane(j)].astype(f32)
            incoming = jnp.where(b < ctx, longer, incoming)
        state_v[:, lane(j)] = incoming

    gate_copy.wait()
    mix_copy.wait()

    def chunk_rows(r):
        return slice(starts[r], starts[r] + sizes[r])

    def mix(r, send=False):
        carried = advance(starts[r], sizes[r], [state_v[:, lane(j)] for j in range(lanes)], True)
        for j in range(lanes):
            state_v[:, lane(j)] = carried[j]
        rows, used = chunk_rows(r), sizes[r] * states
        readout = jnp.dot(select_v[rows, :used], history[:used, :], preferred_element_type=f32)
        gate = gate_v[rows, :].astype(f32)
        signal = mamba_v[rows, :].astype(f32)
        gated = (readout + skip_ref[...] * signal) * (gate / (1.0 + jnp.exp(-gate)))
        gated = gated.astype(bf16)
        to = direct if r == 0 else mixed[r - 1]
        wide = to.shape[2]
        for d in (4, 3, 5, 2, 6, 1, 7, 0) if r == 0 else (2, 1, 3, 0):
            peer = lax.rem(place + d, places) if r == 0 else lax.rem(exp + d, experts)
            here = pl.ds(pl.multiple_of(peer * wide, wide), wide)
            to[peer] = jnp.dot(gated, mix_v[:, here], preferred_element_type=f32).astype(bf16)
            if send and d > 0:
                (direct_copy(d) if r == 0 else z_copy(r, d)).start()

    def direct_copy(d):
        peer, device = member(d)
        return remote(
            direct.at[peer], direct_inbox.at[d - 1], d_send.at[d - 1], d_recv.at[d - 1], device
        )

    def spread_copy(d):
        here = tokens[0].at[ctx, place]
        return remote(here, here, b_send.at[d - 1], b_recv.at[d - 1], member(d)[1])

    def z_copy(r, d):
        peer = z_peers[d - 1]
        return remote(
            mixed[r - 1].at[peer], z_inbox[r - 1].at[d - 1], z_send.at[r - 1, d - 1],
            z_recv.at[r - 1, d - 1], {"exp": peer},
        )

    def y_copy(r):
        return remote(
            y_outbox[r - 1], y_inbox[r - 1], y_send.at[r - 1], y_recv.at[r - 1], {"tp": 1 - tp}
        )

    def a_copy(r, d):
        here = tokens[r].at[ctx, exp]
        return remote(
            here, here, a_send.at[r - 1, d - 1], a_recv.at[r - 1, d - 1], {"exp": z_peers[d - 1]}
        )

    def c_copy(r, n):
        here = tokens[r].at[(ctx, ctx, ctx_peers[1])[n]]
        return remote(
            here, here, c_send.at[r, n], c_recv.at[r, n], {"ctx": ctx_peers[(0, 1, 0)[n]]}
        )

    def scatter(r):
        for d in (2, 1, 3):
            z_copy(r, d).start()

    def swap(r):
        lifted = residual_ref[chunk_rows(r), :].astype(f32)
        total = jnp.concatenate(
            [jnp.where(tp == n, lifted, 0.0) for n in range(2)], axis=1
        ) + mixed[r - 1][exp].astype(f32)
        for d in range(1, experts):
            z_copy(r, d).wait_recv()
            total = total + z_inbox[r - 1][d - 1].astype(f32)
        y_outbox[r - 1][...] = total.astype(bf16)
        y_copy(r).start()

    def gather(r):
        if r == 0:
            total = residual_ref[chunk_rows(r), :].astype(f32) + direct[place].astype(f32)
            for d in range(1, places):
                direct_copy(d).wait_recv()
                total = total + direct_inbox[d - 1].astype(f32)
            gain = gain_ref[:, pl.ds(pl.multiple_of(place * width, width), width)]
            tokens[r][ctx, place] = (total * gain).astype(bf16)
            for d in (4, 3, 5, 2, 6, 1, 7):
                spread_copy(d).start()
        else:
            y_copy(r).wait_recv()
            total = y_outbox[r - 1][...].astype(f32) + y_inbox[r - 1][...].astype(f32)
            gain = gain_ref[:, pl.ds(pl.multiple_of(exp * span, span), span)]
            tokens[r][ctx, exp] = (total * gain).astype(bf16)
            for d in (2, 1, 3):
                a_copy(r, d).start()

    def share(r):
        if r == 0:
            for d in range(1, places):
                spread_copy(d).wait_recv()
        else:
            for d in range(1, experts):
                a_copy(r, d).wait_recv()
        c_copy(r, 0).start()
        c_copy(r, 1).start()

    def relay(r):
        c_copy(r, 1).wait_recv()
        c_copy(r, 2).start()

    near = pl.multiple_of(ctx // 2 * 2, 2)
    passes = hidden_passes(chunks)

    def blocks_of(p):
        kind = passes[p][1]
        return ((near, 2), (2 - near, 2), (0, blocks))[kind]

    def unit_rows(p, r):
        first, count = blocks_of(p)
        return pl.ds(pl.multiple_of(first * sizes[r], 16), count * sizes[r])

    def unit_tokens(p, r, z):
        first, count = blocks_of(p)
        return tokens[r][pl.ds(first, count), z].reshape(count * sizes[r], tokens[r].shape[3])

    def hidden_copy(p, r, k):
        return remote(
            own[r].at[k, unit_rows(p, r)], other[r].at[k, unit_rows(p, r)],
            h_send.at[p, r, k], h_recv.at[p, r, k], {"tp": 1 - tp},
        )

    def measure(p):
        low = 0
        for r in passes[p][0]:
            count = blocks_of(p)[1] * sizes[r]
            squares = jnp.zeros((count, 1), f32)
            for z in range(tokens[r].shape[1]):
                wide = tokens[r].shape[3]
                inverse = 1.0 / gain_ref[:, z * wide : (z + 1) * wide]
                plain = unit_tokens(p, r, z).astype(f32) * inverse
                squares = squares + jnp.sum(plain * plain, axis=1, keepdims=True)
            scale = lax.rsqrt(squares / depth + 1e-06)
            scale_v[low : low + count, :] = jnp.broadcast_to(scale, (count, 128))
            low += count

    def hidden(p, low, high):
        rows_here = sum(blocks_of(p)[1] * sizes[r] for r in passes[p][0])

        def one(k, unused):
            if p == 0:
                wg_copy(k).wait()
                wu_copy(k).wait()
            rows = jnp.concatenate(
                [
                    jnp.concatenate(
                        [unit_tokens(p, r, z) for z in range(tokens[r].shape[1])], axis=1
                    )
                    for r in passes[p][0]
                ],
                axis=0,
            )
            scale = jnp.concatenate([scale_v[:rows_here, :]] * (TILE // 128), axis=1)
            gate = jnp.dot(rows, wg[k], preferred_element_type=f32) * scale
            up = jnp.dot(rows, wu[k], preferred_element_type=f32) * scale
            result = (gate / (1.0 + jnp.exp(-gate)) * up).astype(bf16)
            first = 0
            for r in passes[p][0]:
                count = blocks_of(p)[1] * sizes[r]
                own[r][k, unit_rows(p, r), :] = result[first : first + count]
                first += count
            hidden_copy(p, passes[p][0][0], k).start()
            return unused

        lax.fori_loop(low, high, one, 0)

    def down_rows(half, k):
        return pl.ds(pl.multiple_of((half * tiles + k) * TILE, TILE), TILE)

    def down_own(r):
        acc[r][...] = jnp.zeros(acc[r].shape, f32)

        def one(k, unused):
            acc[r][...] += jnp.dot(
                own[r][k], wd[down_rows(tp, k), :], preferred_element_type=f32
            )
            return unused

        lax.fori_loop(0, tiles, one, 0)

    def part_copy(r, n):
        peer = ctx_peers[n]
        return remote(
            part[r].at[peer], inbox[r].at[n], r_send.at[r, n], r_recv.at[r, n], {"ctx": peer}
        )

    def down_other(r):
        def one(k, unused):
            for p in range(len(passes)):
                if r in passes[p][0]:
                    hidden_copy(p, r, k).wait_recv()
            acc[r][...] += jnp.dot(
                other[r][k], wd[down_rows(1 - tp, k), :], preferred_element_type=f32
            )
            return unused

        lax.fori_loop(0, tiles, one, 0)
        part[r][...] = acc[r][...].astype(bf16).reshape(part[r].shape)
        for n in (1, 2, 0):
            part_copy(r, n).start()

    def finish(r):
        total = acc[r][pl.ds(pl.multiple_of(ctx * sizes[r], 16), sizes[r]), :]
        for n in range(blocks - 1):
            part_copy(r, n).wait_recv()
            total = total + inbox[r][n].astype(f32)
        out_ref[chunk_rows(r), :] = total.astype(out_ref.dtype)

    third, half = tiles // 3, (tiles + 1) // 2
    mix(0, True)
    wd_copy.start()
    mix(1, True)
    mix(2)
    gather(0)
    mix(3)
    swap(1)
    share(0)
    scatter(2)
    c_copy(0, 0).wait_recv()
    measure(0)
    hidden(0, 0, third)
    gather(1)
    relay(0)
    hidden(0, third, 2 * third)
    swap(2)
    scatter(3)
    hidden(0, 2 * third, tiles)
    c_copy(0, 2).wait_recv()
    measure(1)
    hidden(1, 0, half)
    share(1)
    gather(2)
    swap(3)
    hidden(1, half, tiles)
    relay(1)
    gather(3)
    c_copy(1, 0).wait_recv()
    c_copy(1, 2).wait_recv()
    measure(2)
    hidden(2, 0, half)
    share(2)
    hidden(2, half, tiles)
    relay(2)
    share(3)
    wd_copy.wait()
    down_own(0)
    c_copy(2, 0).wait_recv()
    c_copy(2, 2).wait_recv()
    measure(3)
    hidden(3, 0, half)
    relay(3)
    hidden(3, half, tiles)
    c_copy(3, 0).wait_recv()
    c_copy(3, 2).wait_recv()
    measure(4)
    hidden(4, 0, tiles)
    down_own(1)
    down_other(0)
    down_own(2)
    down_other(1)
    down_own(3)
    finish(0)
    down_other(2)
    finish(1)
    down_other(3)
    finish(2)
    finish(3)

    for copy in end_copies:
        copy.wait_send()
    for d in range(1, places):
        direct_copy(d).wait_send()
        spread_copy(d).wait_send()
    for r in range(chunks):
        for n in range(blocks - 1):
            part_copy(r, n).wait_send()
            c_copy(r, n).wait_send()
        if r > 0:
            y_copy(r).wait_send()
            for d in range(1, experts):
                z_copy(r, d).wait_send()
                a_copy(r, d).wait_send()

    def drain(k, unused):
        for p in range(len(passes)):
            for r in passes[p][0]:
                hidden_copy(p, r, k).wait_send()
        return unused

    lax.fori_loop(0, tiles, drain, 0)


def fused(
    mamba_in, gate_in, step_size, input_proj, output_proj, decay_log, skip_gain,
    out_weight, residual, norm_gain, w_gate, w_up, w_down,
):
    length, channels = mamba_in.shape
    states = decay_log.shape[0]
    depth = out_weight.shape[1]
    experts, blocks = lax.axis_size("exp"), lax.axis_size("ctx")
    hidden, width = w_gate.shape[2], w_down.shape[2]
    span, tiles = depth // experts, hidden // TILE
    sizes = chunk_sizes(length)
    chunks, longest, places = len(sizes), max(sizes), 2 * experts
    bf16, f32, dma = jnp.bfloat16, jnp.float32, pltpu.SemaphoreType.DMA
    vmem, anywhere = pl.BlockSpec(memory_space=pltpu.VMEM), pl.BlockSpec(memory_space=pl.ANY)
    passes = hidden_passes(chunks)
    widest = max(
        sum((blocks if kind == 2 else 2) * sizes[r] for r in which) for which, kind in passes
    )
    later = sizes[1:]
    scratch = [
        pltpu.VMEM((length, channels), f32),
        pltpu.VMEM((length, channels), bf16),
        pltpu.VMEM((length, channels), bf16),
        pltpu.VMEM((length, channels), f32),
        pltpu.VMEM((states, channels), f32),
        pltpu.VMEM((length, states, 128), f32),
        pltpu.VMEM((length, longest * states), bf16),
        pltpu.VMEM((longest * states, channels), bf16),
        pltpu.VMEM((states, channels), f32),
        pltpu.VMEM((blocks, states, channels), bf16),
        pltpu.VMEM((blocks, 8, 128), f32),
        pltpu.VMEM((channels, depth), bf16),
        pltpu.VMEM((tiles, depth, TILE), bf16),
        pltpu.VMEM((tiles, depth, TILE), bf16),
        pltpu.VMEM((2 * hidden, width), bf16),
        pltpu.VMEM((widest, 128), f32),
        pltpu.VMEM((places, sizes[0], span // 2), bf16),
        pltpu.VMEM((places - 1, sizes[0], span // 2), bf16),
        [pltpu.VMEM((experts, size, span), bf16) for size in later],
        [pltpu.VMEM((experts - 1, size, span), bf16) for size in later],
        [pltpu.VMEM((size, span), bf16) for size in later],
        [pltpu.VMEM((size, span), bf16) for size in later],
        [pltpu.VMEM((blocks, places, sizes[0], span // 2), bf16)]
        + [pltpu.VMEM((blocks, experts, size, span), bf16) for size in later],
        [pltpu.VMEM((tiles, blocks * size, TILE), bf16) for size in sizes],
        [pltpu.VMEM((tiles, blocks * size, TILE), bf16) for size in sizes],
        [pltpu.VMEM((blocks * size, width), f32) for size in sizes],
        [pltpu.VMEM((blocks, size, width), bf16) for size in sizes],
        [pltpu.VMEM((blocks - 1, size, width), bf16) for size in sizes],
        dma((5,)),
        dma((tiles,)),
        dma((tiles,)),
        dma((blocks - 1,)),
        dma((blocks - 1,)),
        dma((blocks - 1,)),
        dma((blocks - 1,)),
        dma((places - 1,)),
        dma((places - 1,)),
        dma((places - 1,)),
        dma((places - 1,)),
        dma((chunks - 1, experts - 1)),
        dma((chunks - 1, experts - 1)),
        dma((chunks - 1,)),
        dma((chunks - 1,)),
        dma((chunks - 1, experts - 1)),
        dma((chunks - 1, experts - 1)),
        dma((chunks, blocks - 1)),
        dma((chunks, blocks - 1)),
        dma((len(passes), chunks, tiles)),
        dma((len(passes), chunks, tiles)),
        dma((chunks, blocks - 1)),
        dma((chunks, blocks - 1)),
    ]
    return pl.pallas_call(
        fused_kernel,
        out_shape=jax.ShapeDtypeStruct((length, width), bf16),
        in_specs=[anywhere] * 3 + [vmem] * 4 + [anywhere] + [vmem] * 2 + [anywhere] * 3,
        out_specs=vmem,
        scratch_shapes=scratch,
        compiler_params=pltpu.CompilerParams(
            collective_id=0, has_side_effects=True, vmem_limit_bytes=60 << 20
        ),
        name="fused",
    )(
        mamba_in, gate_in, step_size, input_proj, output_proj, decay_log, skip_gain[None, :],
        out_weight, residual, norm_gain[None, :], w_gate, w_up, w_down,
    )


def place_kernel(rows_ref, routes_ref, out_ref):
    mine = lax.axis_index("exp")
    length = rows_ref.shape[0]
    shape = (length, length)
    named = jnp.zeros((1, length), jnp.float32)
    for k in range(routes_ref.shape[0]):
        named = named + jnp.where(routes_ref[k : k + 1, :] == mine, 1.0, 0.0)
    row = lax.broadcasted_iota(jnp.int32, shape, 0)
    column = lax.broadcasted_iota(jnp.int32, shape, 1)
    before = jnp.where(row < column, 1.0, 0.0).astype(jnp.bfloat16)
    tall = jnp.broadcast_to(named, (16, length)).astype(jnp.bfloat16)
    slot = jnp.dot(tall, before, preferred_element_type=jnp.float32)[:1]
    pick = jnp.where(slot == row.astype(jnp.float32), named, 0.0).astype(jnp.bfloat16)
    out_ref[...] = jnp.dot(
        pick, rows_ref[...], preferred_element_type=jnp.float32
    ).astype(out_ref.dtype)


def placed_rows(rows, routes):
    vmem = pl.BlockSpec(memory_space=pltpu.VMEM)
    return pl.pallas_call(
        place_kernel,
        out_shape=jax.ShapeDtypeStruct(rows.shape, rows.dtype),
        in_specs=[vmem] * 2,
        out_specs=vmem,
        name="place",
    )(rows, routes.T)


def scanned_small(mamba_in, gate_in, step_size, input_proj, output_proj, decay_log, skip_gain):
    decay_rate = -jnp.exp(decay_log)
    signal = mamba_in.astype(jnp.float32)
    decays = jnp.exp(step_size[:, None, :] * decay_rate[None, :, :])
    driving = (step_size * signal)[:, None, :] * jnp.transpose(input_proj)[:, :, None]
    cum_decay, local_state = lax.associative_scan(combine_link, (decays, driving), axis=0)
    summary = (cum_decay[-1], local_state[-1])
    identity = (jnp.ones_like(summary[0]), jnp.zeros_like(summary[1]))
    prefix = prefix_2(summary, "ctx", combine_link, identity)
    incoming = prefix[1]
    full_state = local_state + cum_decay * incoming[None, :, :]
    readout = jnp.sum(jnp.transpose(output_proj)[:, :, None] * full_state, axis=1)
    return ((readout + skip_gain * signal) * jax.nn.silu(gate_in.astype(jnp.float32))).astype(
        jnp.bfloat16
    )


def body(
    mamba_in,
    gate_in,
    step_size,
    input_proj,
    output_proj,
    decay_log,
    skip_gain,
    out_weight,
    residual,
    routes,
    norm_gain,
    w_gate,
    w_up,
    w_down,
):
    length = mamba_in.shape[0]
    experts = lax.axis_size("exp")
    top_count = routes.shape[1]
    capacity = length * top_count * 2 // experts
    if fits(mamba_in, out_weight, residual, w_gate, w_down, capacity):
        total = fused(
            mamba_in, gate_in, step_size, input_proj, output_proj, decay_log, skip_gain,
            out_weight, residual, norm_gain, w_gate, w_up, w_down,
        )
        return placed_rows(total, routes)[None, None]
    gated_out = scanned_small(
        mamba_in, gate_in, step_size, input_proj, output_proj, decay_log, skip_gain
    )
    row_ids = route_rows(routes, capacity, experts)
    rows_here = capacity // lax.axis_size("tp")
    col_width = residual.shape[1]
    model_width = out_weight.shape[1]
    offset = lax.axis_index(("exp", "tp")) * col_width
    mixed_rows = jnp.dot(gated_out, out_weight, preferred_element_type=jnp.float32)
    lifted = residual.astype(jnp.float32)
    placed = jnp.zeros((lifted.shape[0], model_width), jnp.float32)
    token_part = lax.psum_scatter(
        mixed_rows + lax.dynamic_update_slice_in_dim(placed, lifted, offset, 1),
        ("exp", "tp"),
        scatter_dimension=0,
        tiled=True,
    )
    every_token = lax.all_gather(
        rms_scale(token_part, norm_gain), ("exp", "tp"), axis=0, tiled=True
    )
    picker = pick_rows(row_ids, lax.axis_index(("exp", "tp")) * rows_here, rows_here)
    normed = jnp.dot(picker, every_token, preferred_element_type=jnp.float32).astype(jnp.bfloat16)
    row_block = lax.all_gather(normed, ("ctx", "tp"), axis=0, tiled=True)
    gate_part = jnp.dot(row_block, w_gate[0], preferred_element_type=jnp.float32)
    up_part = jnp.dot(row_block, w_up[0], preferred_element_type=jnp.float32)
    hidden = (jax.nn.silu(gate_part) * up_part).astype(jnp.bfloat16)
    local_down = w_down[0]
    partial_out = jnp.dot(
        lax.all_gather(hidden, "tp", axis=1, tiled=True),
        local_down,
        preferred_element_type=jnp.float32,
    )
    result = lax.psum_scatter(
        partial_out.astype(jnp.bfloat16), "ctx", scatter_dimension=0, tiled=True
    )
    return result[None, None]


def solution(mesh):
    in_specs = (
        P("ctx", ("exp", "tp")),
        P("ctx", ("exp", "tp")),
        P("ctx", ("exp", "tp")),
        P(None, "ctx"),
        P(None, "ctx"),
        P(None, ("exp", "tp")),
        P(("exp", "tp")),
        P(("exp", "tp"), None),
        P("ctx", ("exp", "tp")),
        P("ctx", None),
        P(),
        P("exp", None, ("ctx", "tp")),
        P("exp", None, ("ctx", "tp")),
        P("exp", "ctx", "tp"),
    )
    out_specs = P("ctx", "exp", None, "tp")
    return jax.shard_map(body, mesh=mesh, in_specs=in_specs, out_specs=out_specs, check_vma=False)
```

```python
import math

import jax
import jax.numpy as jnp
from jax import lax
from jax.experimental import pallas as pl
from jax.experimental.pallas import tpu as pltpu
from jax.sharding import PartitionSpec as P

MESH = pl.DeviceIdType.MESH
LOG2E = math.log2(math.e)
CHUNKS = (2, 2, 2, 2)
TILE = 256


def prefix_2(value, axis, join, neutral):
    count, mine = (lax.axis_size(axis), lax.axis_index(axis))
    pieces = jax.tree.map(lambda part: lax.all_gather(part, axis), value)
    so_far = jax.tree.map(
        lambda part, zero: jnp.full_like(part, 0) + jnp.asarray(zero, part.dtype), value, neutral
    )

    def step(position, so_far):
        longer = join(so_far, jax.tree.map(lambda part: part[position], pieces))
        return jax.tree.map(lambda new, old: jnp.where(position < mine, new, old), longer, so_far)

    return lax.fori_loop(0, count - 1, step, so_far)


def route_rows(routes, capacity, experts):
    flattened = routes.reshape(-1)
    one_hot = (flattened[:, None] == jnp.arange(experts, dtype=jnp.int32)[None, :]).astype(
        jnp.float32
    )
    pairs = jnp.arange(flattened.shape[0], dtype=jnp.int32)
    before = (pairs[None, :] < pairs[:, None]).astype(jnp.float32)
    earlier = jnp.dot(before, one_hot, preferred_element_type=jnp.float32)
    slot_index = jnp.sum(earlier * one_hot, axis=1).astype(jnp.int32)
    return (flattened * capacity + slot_index).reshape(routes.shape)


def pick_rows(row_ids, first_row, row_count):
    targets = first_row + jnp.arange(row_count, dtype=jnp.int32)
    matches = row_ids[None, :, :] == targets[:, None, None]
    return jnp.sum(matches.astype(jnp.float32), axis=2).astype(jnp.bfloat16)


def rms_scale(row_data, norm_gain):
    mean_sq = jnp.mean(row_data * row_data, axis=1, keepdims=True)
    return (row_data * lax.rsqrt(mean_sq + 1e-06) * norm_gain).astype(jnp.bfloat16)


def combine_link(earlier, later_link):
    return (earlier[0] * later_link[0], later_link[0] * earlier[1] + later_link[1])


def fits(mamba_in, out_weight, residual, w_gate, w_down, capacity):
    length, channels = mamba_in.shape
    depth = out_weight.shape[1]
    experts = lax.axis_size("exp")
    return (
        lax.axis_size("tp") == 2
        and lax.axis_size("ctx") == 4
        and experts == 4
        and channels % 128 == 0
        and channels // 128 <= 8
        and capacity == length
        and length % 128 == 0
        and depth % (2 * experts * 128) == 0
        and w_gate.shape[2] % TILE == 0
        and w_down.shape[0] == 1
    )


def chunk_sizes(length):
    part = length // 8
    return tuple(n * part for n in CHUNKS)


def hidden_passes(chunks):
    return [((0,), 0), ((0,), 1)] + [((r,), 2) for r in range(1, chunks)]


def fused_kernel(
    mamba_hbm, gate_hbm, step_hbm, in_hbm, read_hbm, decay_hbm, skip_hbm, mix_hbm,
    residual_hbm, gain_hbm, wg_hbm, wu_hbm, wd_hbm, out_ref,
    in_ref, read_ref, decay_ref, skip_ref, residual_ref, gain_ref,
    step_v, mamba_v, gate_v, drive_v, rate_v, spread_v, select_v, history, state_v,
    ends, totals, mix_v, wg, wu, wd,
    scale_v, direct, direct_inbox, mixed, z_inbox, y_outbox, y_inbox, tokens, own, other, acc,
    part, inbox,
    load_sem, small_sem, g_sem, u_sem, e_send, e_recv, t_send, t_recv, d_send, d_recv, b_send, b_recv,
    z_send, z_recv, y_send, y_recv, a_send, a_recv, c_send, c_recv, h_send, h_recv,
    r_send, r_recv,
):
    ctx, exp, tp = lax.axis_index("ctx"), lax.axis_index("exp"), lax.axis_index("tp")
    experts = lax.axis_size("exp")
    blocks = lax.axis_size("ctx")
    length, channels = step_v.shape
    states = rate_v.shape[0]
    sizes = chunk_sizes(length)
    starts = [sum(sizes[:r]) for r in range(len(sizes))]
    chunks = len(sizes)
    longest = max(sizes)
    lanes = channels // 128
    span = tokens[-1].shape[-1]
    width = span // 2
    depth = span * experts
    tiles = wg.shape[0]
    bf16, f32 = jnp.bfloat16, jnp.float32

    ctx_peers = (ctx + 1 - 2 * lax.rem(ctx, 2), lax.rem(ctx + 2, blocks), blocks - 1 - ctx)
    z_peers = [lax.rem(exp + d, experts) for d in range(1, experts)]

    barrier = pltpu.get_barrier_semaphore()
    place, places = exp * 2 + tp, 2 * experts

    def member(d):
        peer = lax.rem(place + d, places)
        return peer, {"exp": peer // 2, "tp": lax.rem(peer, 2)}

    greeted = [member(d)[1] for d in range(1, places)] + [{"ctx": c} for c in ctx_peers]
    for device in greeted:
        pl.semaphore_signal(barrier, inc=1, device_id=device, device_id_type=MESH)

    def remote(src, dst, send_sem, recv_sem, device):
        return pltpu.make_async_remote_copy(
            src_ref=src, dst_ref=dst, send_sem=send_sem, recv_sem=recv_sem,
            device_id=device, device_id_type=MESH,
        )

    step_copy = pltpu.make_async_copy(step_hbm, step_v, load_sem.at[0])
    mamba_copy = pltpu.make_async_copy(mamba_hbm, mamba_v, load_sem.at[1])
    gate_copy = pltpu.make_async_copy(gate_hbm, gate_v, load_sem.at[2])
    mix_copy = pltpu.make_async_copy(mix_hbm, mix_v, load_sem.at[3])
    wd_copy = pltpu.make_async_copy(wd_hbm.at[0], wd, load_sem.at[4])

    def columns(k):
        return pl.ds(pl.multiple_of(k * TILE, TILE), TILE)

    def wg_copy(k):
        return pltpu.make_async_copy(wg_hbm.at[0, :, columns(k)], wg.at[k], g_sem.at[k])

    def wu_copy(k):
        return pltpu.make_async_copy(wu_hbm.at[0, :, columns(k)], wu.at[k], u_sem.at[k])

    small = [
        pltpu.make_async_copy(src, dst, small_sem.at[n])
        for n, (src, dst) in enumerate(
            (
                (in_hbm, in_ref), (decay_hbm, decay_ref), (read_hbm, read_ref),
                (skip_hbm, skip_ref), (residual_hbm, residual_ref), (gain_hbm, gain_ref),
            )
        )
    ]
    for copy in small[:2]:
        copy.start()
    step_copy.start()
    mamba_copy.start()
    for copy in small[2:]:
        copy.start()
    for copy in small[:2]:
        copy.wait()

    rate_v[...] = -jnp.exp(decay_ref[...]) * LOG2E
    for t in range(length):
        spread_v[t] = jnp.broadcast_to(in_ref[:, t : t + 1], (states, 128))
    step_copy.wait()
    mamba_copy.wait()
    gate_copy.start()
    mix_copy.start()
    drive_v[...] = mamba_v[...].astype(f32) * step_v[...]

    def lane(j):
        return slice(j * 128, (j + 1) * 128)

    def advance(first, count, carried, keep):
        rates = [rate_v[:, lane(j)] for j in range(lanes)]

        def eight(g, carried):
            carried = list(carried)
            base = pl.multiple_of(first + g * 8, 8)
            steps = [step_v[pl.ds(base, 8), lane(j)] for j in range(lanes)]
            drives = [drive_v[pl.ds(base, 8), lane(j)] for j in range(lanes)]
            for i in range(8):
                spread = spread_v[base + i]
                for j in range(lanes):
                    step = jnp.broadcast_to(steps[j][i : i + 1], (states, 128))
                    drive = jnp.broadcast_to(drives[j][i : i + 1], (states, 128))
                    carried[j] = jnp.exp2(step * rates[j]) * carried[j] + drive * spread
                    if keep:
                        row = pl.multiple_of((g * 8 + i) * states, states)
                        history[pl.ds(row, states), lane(j)] = carried[j].astype(bf16)
            return tuple(carried)

        return lax.fori_loop(0, count // 8, eight, tuple(carried))

    local = advance(0, length, (jnp.zeros((states, 128), f32),) * lanes, False)
    sums = jnp.sum(step_v[...], axis=0, keepdims=True)
    for j in range(lanes):
        ends[ctx, :, lane(j)] = local[j].astype(bf16)
        totals[ctx, j : j + 1, :] = sums[:, lane(j)]

    pl.semaphore_wait(barrier, len(greeted))
    end_copies = []
    for n, peer in enumerate(ctx_peers):
        end_copies.append(
            remote(ends.at[ctx], ends.at[ctx], e_send.at[n], e_recv.at[n], {"ctx": peer})
        )
        end_copies.append(
            remote(totals.at[ctx], totals.at[ctx], t_send.at[n], t_recv.at[n], {"ctx": peer})
        )
    for copy in end_copies:
        copy.start()
    for k in range(tiles):
        wg_copy(k).start()
        wu_copy(k).start()

    for copy in small[2:]:
        copy.wait()
    column = lax.broadcasted_iota(jnp.int32, (states, longest * states), 1)
    row = lax.broadcasted_iota(jnp.int32, (states, longest * states), 0)
    repeat = jnp.where(lax.rem(column, states) == row, 1.0, 0.0).astype(bf16)
    wide = lax.dot_general(
        read_ref[...].astype(bf16), repeat, (((0,), (0,)), ((), ())), preferred_element_type=f32
    )
    for r in range(chunks):
        shape = (sizes[r], longest * states)
        position = lax.broadcasted_iota(jnp.int32, shape, 0)
        owner = lax.broadcasted_iota(jnp.int32, shape, 1) // states
        rows = slice(starts[r], starts[r] + sizes[r])
        select_v[rows, :] = jnp.where(position == owner, wide[rows, :], 0.0).astype(bf16)

    for copy in end_copies:
        copy.wait_recv()
    for j in range(lanes):
        rate = rate_v[:, lane(j)]
        incoming = jnp.zeros((states, 128), f32)
        for b in range(blocks - 1):
            total = jnp.broadcast_to(totals[b, j : j + 1, :], (states, 128))
            longer = jnp.exp2(total * rate) * incoming + ends[b, :, lane(j)].astype(f32)
            incoming = jnp.where(b < ctx, longer, incoming)
        state_v[:, lane(j)] = incoming

    gate_copy.wait()
    mix_copy.wait()

    def chunk_rows(r):
        return slice(starts[r], starts[r] + sizes[r])

    def mix(r, send=False):
        carried = advance(starts[r], sizes[r], [state_v[:, lane(j)] for j in range(lanes)], True)
        for j in range(lanes):
            state_v[:, lane(j)] = carried[j]
        rows, used = chunk_rows(r), sizes[r] * states
        readout = jnp.dot(select_v[rows, :used], history[:used, :], preferred_element_type=f32)
        gate = gate_v[rows, :].astype(f32)
        signal = mamba_v[rows, :].astype(f32)
        gated = (readout + skip_ref[...] * signal) * (gate / (1.0 + jnp.exp(-gate)))
        gated = gated.astype(bf16)
        to = direct if r == 0 else mixed[r - 1]
        wide = to.shape[2]
        for d in (4, 3, 5, 2, 6, 1, 7, 0) if r == 0 else (2, 1, 3, 0):
            peer = lax.rem(place + d, places) if r == 0 else lax.rem(exp + d, experts)
            here = pl.ds(pl.multiple_of(peer * wide, wide), wide)
            to[peer] = jnp.dot(gated, mix_v[:, here], preferred_element_type=f32).astype(bf16)
            if send and d > 0:
                (direct_copy(d) if r == 0 else z_copy(r, d)).start()

    def direct_copy(d):
        peer, device = member(d)
        return remote(
            direct.at[peer], direct_inbox.at[d - 1], d_send.at[d - 1], d_recv.at[d - 1], device
        )

    def spread_copy(d):
        here = tokens[0].at[ctx, place]
        return remote(here, here, b_send.at[d - 1], b_recv.at[d - 1], member(d)[1])

    def z_copy(r, d):
        peer = z_peers[d - 1]
        return remote(
            mixed[r - 1].at[peer], z_inbox[r - 1].at[d - 1], z_send.at[r - 1, d - 1],
            z_recv.at[r - 1, d - 1], {"exp": peer},
        )

    def y_copy(r):
        return remote(
            y_outbox[r - 1], y_inbox[r - 1], y_send.at[r - 1], y_recv.at[r - 1], {"tp": 1 - tp}
        )

    def a_copy(r, d):
        here = tokens[r].at[ctx, exp]
        return remote(
            here, here, a_send.at[r - 1, d - 1], a_recv.at[r - 1, d - 1], {"exp": z_peers[d - 1]}
        )

    def c_copy(r, n):
        here = tokens[r].at[(ctx, ctx, ctx_peers[1])[n]]
        return remote(
            here, here, c_send.at[r, n], c_recv.at[r, n], {"ctx": ctx_peers[(0, 1, 0)[n]]}
        )

    def scatter(r):
        for d in (2, 1, 3):
            z_copy(r, d).start()

    def swap(r):
        lifted = residual_ref[chunk_rows(r), :].astype(f32)
        total = jnp.concatenate(
            [jnp.where(tp == n, lifted, 0.0) for n in range(2)], axis=1
        ) + mixed[r - 1][exp].astype(f32)
        for d in range(1, experts):
            z_copy(r, d).wait_recv()
            total = total + z_inbox[r - 1][d - 1].astype(f32)
        y_outbox[r - 1][...] = total.astype(bf16)
        y_copy(r).start()

    def gather(r):
        if r == 0:
            total = residual_ref[chunk_rows(r), :].astype(f32) + direct[place].astype(f32)
            for d in range(1, places):
                direct_copy(d).wait_recv()
                total = total + direct_inbox[d - 1].astype(f32)
            gain = gain_ref[:, pl.ds(pl.multiple_of(place * width, width), width)]
            tokens[r][ctx, place] = (total * gain).astype(bf16)
            for d in (4, 3, 5, 2, 6, 1, 7):
                spread_copy(d).start()
        else:
            y_copy(r).wait_recv()
            total = y_outbox[r - 1][...].astype(f32) + y_inbox[r - 1][...].astype(f32)
            gain = gain_ref[:, pl.ds(pl.multiple_of(exp * span, span), span)]
            tokens[r][ctx, exp] = (total * gain).astype(bf16)
            for d in (2, 1, 3):
                a_copy(r, d).start()

    def share(r):
        if r == 0:
            for d in range(1, places):
                spread_copy(d).wait_recv()
        else:
            for d in range(1, experts):
                a_copy(r, d).wait_recv()
        c_copy(r, 0).start()
        c_copy(r, 1).start()

    def relay(r):
        c_copy(r, 1).wait_recv()
        c_copy(r, 2).start()

    near = pl.multiple_of(ctx // 2 * 2, 2)
    passes = hidden_passes(chunks)

    def blocks_of(p):
        kind = passes[p][1]
        return ((near, 2), (2 - near, 2), (0, blocks))[kind]

    def unit_rows(p, r):
        first, count = blocks_of(p)
        return pl.ds(pl.multiple_of(first * sizes[r], 16), count * sizes[r])

    def unit_tokens(p, r, z):
        first, count = blocks_of(p)
        return tokens[r][pl.ds(first, count), z].reshape(count * sizes[r], tokens[r].shape[3])

    def hidden_copy(p, r, k):
        return remote(
            own[r].at[k, unit_rows(p, r)], other[r].at[k, unit_rows(p, r)],
            h_send.at[p, r, k], h_recv.at[p, r, k], {"tp": 1 - tp},
        )

    def measure(p):
        low = 0
        for r in passes[p][0]:
            count = blocks_of(p)[1] * sizes[r]
            squares = jnp.zeros((count, 1), f32)
            for z in range(tokens[r].shape[1]):
                wide = tokens[r].shape[3]
                inverse = 1.0 / gain_ref[:, z * wide : (z + 1) * wide]
                plain = unit_tokens(p, r, z).astype(f32) * inverse
                squares = squares + jnp.sum(plain * plain, axis=1, keepdims=True)
            scale = lax.rsqrt(squares / depth + 1e-06)
            scale_v[low : low + count, :] = jnp.broadcast_to(scale, (count, 128))
            low += count

    def hidden(p, low, high):
        rows_here = sum(blocks_of(p)[1] * sizes[r] for r in passes[p][0])

        def one(k, unused):
            if p == 0:
                wg_copy(k).wait()
                wu_copy(k).wait()
            rows = jnp.concatenate(
                [
                    jnp.concatenate(
                        [unit_tokens(p, r, z) for z in range(tokens[r].shape[1])], axis=1
                    )
                    for r in passes[p][0]
                ],
                axis=0,
            )
            scale = jnp.concatenate([scale_v[:rows_here, :]] * (TILE // 128), axis=1)
            gate = jnp.dot(rows, wg[k], preferred_element_type=f32) * scale
            up = jnp.dot(rows, wu[k], preferred_element_type=f32) * scale
            result = (gate / (1.0 + jnp.exp(-gate)) * up).astype(bf16)
            first = 0
            for r in passes[p][0]:
                count = blocks_of(p)[1] * sizes[r]
                own[r][k, unit_rows(p, r), :] = result[first : first + count]
                first += count
            hidden_copy(p, passes[p][0][0], k).start()
            return unused

        lax.fori_loop(low, high, one, 0)

    def down_rows(half, k):
        return pl.ds(pl.multiple_of((half * tiles + k) * TILE, TILE), TILE)

    def down_own(r):
        acc[r][...] = jnp.zeros(acc[r].shape, f32)

        def one(k, unused):
            acc[r][...] += jnp.dot(
                own[r][k], wd[down_rows(tp, k), :], preferred_element_type=f32
            )
            return unused

        lax.fori_loop(0, tiles, one, 0)

    def part_copy(r, n):
        peer = ctx_peers[n]
        return remote(
            part[r].at[peer], inbox[r].at[n], r_send.at[r, n], r_recv.at[r, n], {"ctx": peer}
        )

    def down_other(r):
        def one(k, unused):
            for p in range(len(passes)):
                if r in passes[p][0]:
                    hidden_copy(p, r, k).wait_recv()
            acc[r][...] += jnp.dot(
                other[r][k], wd[down_rows(1 - tp, k), :], preferred_element_type=f32
            )
            return unused

        lax.fori_loop(0, tiles, one, 0)
        part[r][...] = acc[r][...].astype(bf16).reshape(part[r].shape)
        for n in (1, 2, 0):
            part_copy(r, n).start()

    def finish(r):
        total = acc[r][pl.ds(pl.multiple_of(ctx * sizes[r], 16), sizes[r]), :]
        for n in range(blocks - 1):
            part_copy(r, n).wait_recv()
            total = total + inbox[r][n].astype(f32)
        out_ref[chunk_rows(r), :] = total.astype(out_ref.dtype)

    third, half = tiles // 3, (tiles + 1) // 2
    mix(0, True)
    wd_copy.start()
    mix(1, True)
    mix(2)
    gather(0)
    mix(3)
    swap(1)
    share(0)
    scatter(2)
    c_copy(0, 0).wait_recv()
    measure(0)
    hidden(0, 0, third)
    gather(1)
    relay(0)
    hidden(0, third, 2 * third)
    swap(2)
    scatter(3)
    hidden(0, 2 * third, tiles)
    c_copy(0, 2).wait_recv()
    measure(1)
    hidden(1, 0, half)
    share(1)
    gather(2)
    swap(3)
    hidden(1, half, tiles)
    relay(1)
    gather(3)
    c_copy(1, 0).wait_recv()
    c_copy(1, 2).wait_recv()
    measure(2)
    hidden(2, 0, half)
    share(2)
    hidden(2, half, tiles)
    relay(2)
    share(3)
    wd_copy.wait()
    down_own(0)
    c_copy(2, 0).wait_recv()
    c_copy(2, 2).wait_recv()
    measure(3)
    hidden(3, 0, half)
    relay(3)
    hidden(3, half, tiles)
    c_copy(3, 0).wait_recv()
    c_copy(3, 2).wait_recv()
    measure(4)
    hidden(4, 0, tiles)
    down_own(1)
    down_other(0)
    down_own(2)
    down_other(1)
    down_own(3)
    finish(0)
    down_other(2)
    finish(1)
    down_other(3)
    finish(2)
    finish(3)

    for copy in end_copies:
        copy.wait_send()
    for d in range(1, places):
        direct_copy(d).wait_send()
        spread_copy(d).wait_send()
    for r in range(chunks):
        for n in range(blocks - 1):
            part_copy(r, n).wait_send()
            c_copy(r, n).wait_send()
        if r > 0:
            y_copy(r).wait_send()
            for d in range(1, experts):
                z_copy(r, d).wait_send()
                a_copy(r, d).wait_send()

    def drain(k, unused):
        for p in range(len(passes)):
            for r in passes[p][0]:
                hidden_copy(p, r, k).wait_send()
        return unused

    lax.fori_loop(0, tiles, drain, 0)


def fused(
    mamba_in, gate_in, step_size, input_proj, output_proj, decay_log, skip_gain,
    out_weight, residual, norm_gain, w_gate, w_up, w_down,
):
    length, channels = mamba_in.shape
    states = decay_log.shape[0]
    depth = out_weight.shape[1]
    experts, blocks = lax.axis_size("exp"), lax.axis_size("ctx")
    hidden, width = w_gate.shape[2], w_down.shape[2]
    span, tiles = depth // experts, hidden // TILE
    sizes = chunk_sizes(length)
    chunks, longest, places = len(sizes), max(sizes), 2 * experts
    bf16, f32, dma = jnp.bfloat16, jnp.float32, pltpu.SemaphoreType.DMA
    vmem, anywhere = pl.BlockSpec(memory_space=pltpu.VMEM), pl.BlockSpec(memory_space=pl.ANY)
    passes = hidden_passes(chunks)
    widest = max(
        sum((blocks if kind == 2 else 2) * sizes[r] for r in which) for which, kind in passes
    )
    later = sizes[1:]
    scratch = [
        pltpu.VMEM((states, length), f32),
        pltpu.VMEM((states, length), f32),
        pltpu.VMEM((states, channels), f32),
        pltpu.VMEM((1, channels), f32),
        pltpu.VMEM((length, depth // (2 * experts)), bf16),
        pltpu.VMEM((1, depth), f32),
        pltpu.VMEM((length, channels), f32),
        pltpu.VMEM((length, channels), bf16),
        pltpu.VMEM((length, channels), bf16),
        pltpu.VMEM((length, channels), f32),
        pltpu.VMEM((states, channels), f32),
        pltpu.VMEM((length, states, 128), f32),
        pltpu.VMEM((length, longest * states), bf16),
        pltpu.VMEM((longest * states, channels), bf16),
        pltpu.VMEM((states, channels), f32),
        pltpu.VMEM((blocks, states, channels), bf16),
        pltpu.VMEM((blocks, 8, 128), f32),
        pltpu.VMEM((channels, depth), bf16),
        pltpu.VMEM((tiles, depth, TILE), bf16),
        pltpu.VMEM((tiles, depth, TILE), bf16),
        pltpu.VMEM((2 * hidden, width), bf16),
        pltpu.VMEM((widest, 128), f32),
        pltpu.VMEM((places, sizes[0], span // 2), bf16),
        pltpu.VMEM((places - 1, sizes[0], span // 2), bf16),
        [pltpu.VMEM((experts, size, span), bf16) for size in later],
        [pltpu.VMEM((experts - 1, size, span), bf16) for size in later],
        [pltpu.VMEM((size, span), bf16) for size in later],
        [pltpu.VMEM((size, span), bf16) for size in later],
        [pltpu.VMEM((blocks, places, sizes[0], span // 2), bf16)]
        + [pltpu.VMEM((blocks, experts, size, span), bf16) for size in later],
        [pltpu.VMEM((tiles, blocks * size, TILE), bf16) for size in sizes],
        [pltpu.VMEM((tiles, blocks * size, TILE), bf16) for size in sizes],
        [pltpu.VMEM((blocks * size, width), f32) for size in sizes],
        [pltpu.VMEM((blocks, size, width), bf16) for size in sizes],
        [pltpu.VMEM((blocks - 1, size, width), bf16) for size in sizes],
        dma((5,)),
        dma((6,)),
        dma((tiles,)),
        dma((tiles,)),
        dma((blocks - 1,)),
        dma((blocks - 1,)),
        dma((blocks - 1,)),
        dma((blocks - 1,)),
        dma((places - 1,)),
        dma((places - 1,)),
        dma((places - 1,)),
        dma((places - 1,)),
        dma((chunks - 1, experts - 1)),
        dma((chunks - 1, experts - 1)),
        dma((chunks - 1,)),
        dma((chunks - 1,)),
        dma((chunks - 1, experts - 1)),
        dma((chunks - 1, experts - 1)),
        dma((chunks, blocks - 1)),
        dma((chunks, blocks - 1)),
        dma((len(passes), chunks, tiles)),
        dma((len(passes), chunks, tiles)),
        dma((chunks, blocks - 1)),
        dma((chunks, blocks - 1)),
    ]
    return pl.pallas_call(
        fused_kernel,
        out_shape=jax.ShapeDtypeStruct((length, width), bf16),
        in_specs=[anywhere] * 13,
        out_specs=vmem,
        scratch_shapes=scratch,
        compiler_params=pltpu.CompilerParams(
            collective_id=0, has_side_effects=True, vmem_limit_bytes=60 << 20
        ),
        name="fused",
    )(
        mamba_in, gate_in, step_size, input_proj, output_proj, decay_log, skip_gain[None, :],
        out_weight, residual, norm_gain[None, :], w_gate, w_up, w_down,
    )


def place_kernel(rows_ref, routes_ref, out_ref):
    mine = lax.axis_index("exp")
    length = rows_ref.shape[0]
    shape = (length, length)
    named = jnp.zeros((1, length), jnp.float32)
    for k in range(routes_ref.shape[0]):
        named = named + jnp.where(routes_ref[k : k + 1, :] == mine, 1.0, 0.0)
    row = lax.broadcasted_iota(jnp.int32, shape, 0)
    column = lax.broadcasted_iota(jnp.int32, shape, 1)
    before = jnp.where(row < column, 1.0, 0.0).astype(jnp.bfloat16)
    tall = jnp.broadcast_to(named, (16, length)).astype(jnp.bfloat16)
    slot = jnp.dot(tall, before, preferred_element_type=jnp.float32)[:1]
    pick = jnp.where(slot == row.astype(jnp.float32), named, 0.0).astype(jnp.bfloat16)
    out_ref[...] = jnp.dot(
        pick, rows_ref[...], preferred_element_type=jnp.float32
    ).astype(out_ref.dtype)


def placed_rows(rows, routes):
    vmem = pl.BlockSpec(memory_space=pltpu.VMEM)
    return pl.pallas_call(
        place_kernel,
        out_shape=jax.ShapeDtypeStruct(rows.shape, rows.dtype),
        in_specs=[vmem] * 2,
        out_specs=vmem,
        name="place",
    )(rows, routes.T)


def scanned_small(mamba_in, gate_in, step_size, input_proj, output_proj, decay_log, skip_gain):
    decay_rate = -jnp.exp(decay_log)
    signal = mamba_in.astype(jnp.float32)
    decays = jnp.exp(step_size[:, None, :] * decay_rate[None, :, :])
    driving = (step_size * signal)[:, None, :] * jnp.transpose(input_proj)[:, :, None]
    cum_decay, local_state = lax.associative_scan(combine_link, (decays, driving), axis=0)
    summary = (cum_decay[-1], local_state[-1])
    identity = (jnp.ones_like(summary[0]), jnp.zeros_like(summary[1]))
    prefix = prefix_2(summary, "ctx", combine_link, identity)
    incoming = prefix[1]
    full_state = local_state + cum_decay * incoming[None, :, :]
    readout = jnp.sum(jnp.transpose(output_proj)[:, :, None] * full_state, axis=1)
    return ((readout + skip_gain * signal) * jax.nn.silu(gate_in.astype(jnp.float32))).astype(
        jnp.bfloat16
    )


def body(
    mamba_in,
    gate_in,
    step_size,
    input_proj,
    output_proj,
    decay_log,
    skip_gain,
    out_weight,
    residual,
    routes,
    norm_gain,
    w_gate,
    w_up,
    w_down,
):
    length = mamba_in.shape[0]
    experts = lax.axis_size("exp")
    top_count = routes.shape[1]
    capacity = length * top_count * 2 // experts
    if fits(mamba_in, out_weight, residual, w_gate, w_down, capacity):
        total = fused(
            mamba_in, gate_in, step_size, input_proj, output_proj, decay_log, skip_gain,
            out_weight, residual, norm_gain, w_gate, w_up, w_down,
        )
        return placed_rows(total, routes)[None, None]
    gated_out = scanned_small(
        mamba_in, gate_in, step_size, input_proj, output_proj, decay_log, skip_gain
    )
    row_ids = route_rows(routes, capacity, experts)
    rows_here = capacity // lax.axis_size("tp")
    col_width = residual.shape[1]
    model_width = out_weight.shape[1]
    offset = lax.axis_index(("exp", "tp")) * col_width
    mixed_rows = jnp.dot(gated_out, out_weight, preferred_element_type=jnp.float32)
    lifted = residual.astype(jnp.float32)
    placed = jnp.zeros((lifted.shape[0], model_width), jnp.float32)
    token_part = lax.psum_scatter(
        mixed_rows + lax.dynamic_update_slice_in_dim(placed, lifted, offset, 1),
        ("exp", "tp"),
        scatter_dimension=0,
        tiled=True,
    )
    every_token = lax.all_gather(
        rms_scale(token_part, norm_gain), ("exp", "tp"), axis=0, tiled=True
    )
    picker = pick_rows(row_ids, lax.axis_index(("exp", "tp")) * rows_here, rows_here)
    normed = jnp.dot(picker, every_token, preferred_element_type=jnp.float32).astype(jnp.bfloat16)
    row_block = lax.all_gather(normed, ("ctx", "tp"), axis=0, tiled=True)
    gate_part = jnp.dot(row_block, w_gate[0], preferred_element_type=jnp.float32)
    up_part = jnp.dot(row_block, w_up[0], preferred_element_type=jnp.float32)
    hidden = (jax.nn.silu(gate_part) * up_part).astype(jnp.bfloat16)
    local_down = w_down[0]
    partial_out = jnp.dot(
        lax.all_gather(hidden, "tp", axis=1, tiled=True),
        local_down,
        preferred_element_type=jnp.float32,
    )
    result = lax.psum_scatter(
        partial_out.astype(jnp.bfloat16), "ctx", scatter_dimension=0, tiled=True
    )
    return result[None, None]


def solution(mesh):
    in_specs = (
        P("ctx", ("exp", "tp")),
        P("ctx", ("exp", "tp")),
        P("ctx", ("exp", "tp")),
        P(None, "ctx"),
        P(None, "ctx"),
        P(None, ("exp", "tp")),
        P(("exp", "tp")),
        P(("exp", "tp"), None),
        P("ctx", ("exp", "tp")),
        P("ctx", None),
        P(),
        P("exp", None, ("ctx", "tp")),
        P("exp", None, ("ctx", "tp")),
        P("exp", "ctx", "tp"),
    )
    out_specs = P("ctx", "exp", None, "tp")
    return jax.shard_map(body, mesh=mesh, in_specs=in_specs, out_specs=out_specs, check_vma=False)
```
